256 devices in a mesh: row: 16 (over y, x), col: 16 (over z, core).
Axes of the slice: x: 4, y: 4, z: 8, core: 2. Of those that a mesh axis runs over, the one named last changes fastest.
Arguments:
- unfolding: float32 [1024, 32768], P('row', 'col'), may hold values from -40 to 40, as said below
- factor: float32 [1024, 64], replicated, may hold values from -6 to 6
Outputs:
- gram_lower: float32 [1024, 1024], P(('row', 'col'))
- new_factor: float32 [1024, 64], replicated
- core: float32 [64, 32768], P('row', 'col')
The draws below stay inside these ranges and needn't reach their ends.
Inputs may be any that keep to these rules, and one draw needn't show every extreme that they name: Entries of the unfolding are real values.
All inputs are finite; a program needn't handle non-finite values.
Results may differ from the reference program's by a relative error of at most 0.0003.
Values sent between devices are 32-bit elements; how exact they have to be, the bound alone decides.
A program may use at most 64 MiB of HBM per device.

```python
import math
import jax
import jax.numpy as jnp
import numpy as np
from jax import lax

M = 1024
RANK = 64
COLS = 32768
HALF = 2
N_ROW = 16
N_COL = 16


def draw_unfolding(key, part):
    base = jax.random.fold_in(key, 11)
    keys = jax.random.split(base, 5)
    noise = jax.random.normal(keys[0], (M, COLS), jnp.float32)
    left = jax.random.normal(keys[1], (M, 16), jnp.float32)
    right = jax.random.normal(keys[2], (16, COLS), jnp.float32)
    weight_common = 0.3
    row_scale = jnp.exp(jax.random.uniform(keys[3], (M,), jnp.float32, math.log(0.5), math.log(3.0)))
    col_scale = jnp.exp(jax.random.uniform(keys[4], (COLS,), jnp.float32, math.log(0.5), math.log(2.0)))
    common = jnp.dot(left, right) * (weight_common / 4.0)
    values = row_scale[:, None] * (noise + common) * col_scale[None, :]
    return jnp.clip(values, -40.0, 40.0)


def bell_draw(key, shape, width, bound, held_as=jnp.bfloat16):
    array = width * jax.random.normal(key, shape, jnp.float32)
    return jnp.clip(array, min=-bound, max=bound).astype(held_as)


def setup_inputs(seed: int = 0) -> dict:
    seeds = jax.random.split(jax.random.key(seed), 3)
    unfolding = draw_unfolding(jax.random.fold_in(seeds[2], 71), 0)
    factor = bell_draw(seeds[1], (M, RANK), 1.0, 6.0, jnp.float32)
    return {"unfolding": unfolding, "factor": factor}


def folded_source(mode, half, devices):
    place = np.arange(mode)
    owner = place // (2 * half)
    inner = place % (2 * half)
    return np.where(inner < half, owner * half + inner, (2 * devices - 1 - owner) * half + inner - half)

def reference(unfolding, factor):
    highest = lax.Precision.HIGHEST
    devices = N_ROW * N_COL
    gram = jnp.dot(unfolding.astype(jnp.float32), unfolding.T.astype(jnp.float32), precision=highest, preferred_element_type=jnp.float32) / COLS
    source = jnp.asarray(folded_source(M, HALF, devices)).astype(jnp.int32)
    picked = gram[source]
    columns = jnp.arange(M, dtype=jnp.int32)
    gram_lower = jnp.where(columns[None, :] <= source[:, None], picked, jnp.float32(0.0))
    image = jnp.dot(gram.astype(jnp.float32), factor.astype(jnp.float32), precision=highest, preferred_element_type=jnp.float32)
    inner = jnp.dot(image.T.astype(jnp.float32), image.astype(jnp.float32), precision=highest, preferred_element_type=jnp.float32) / M
    chol = jnp.linalg.cholesky(inner)
    new_factor = jax.scipy.linalg.solve_triangular(chol, image.T, lower=True).T
    core = jnp.dot(new_factor.T.astype(jnp.float32), unfolding.astype(jnp.float32), precision=highest, preferred_element_type=jnp.float32) / math.sqrt(M)
    return (gram_lower, new_factor, core)
```

```python
import functools
import math

import jax
import jax.numpy as jnp
from jax import lax
from jax.experimental import pallas as pl
from jax.experimental.pallas import tpu as pltpu
from jax.sharding import PartitionSpec as P

F32 = jnp.float32
BF16 = jnp.bfloat16
HIGHEST = lax.Precision.HIGHEST
MESH = pl.DeviceIdType.MESH

NY, NX, NZ, NK = 4, 4, 8, 2
NR = NY * NX
MODE, RANK, COLS = 1024, 64, 32768
ROWS = MODE // NR
LANES = 128
GW = 1152

PLANE = [(oy, ox) for oy in range(NY) for ox in range(NX) if (oy, ox) != (0, 0)]
PLANE.sort(key=lambda o: -(min(o[0], NY - o[0]) + min(o[1], NX - o[1])))
PLANE_K = [(oy, ox, ok) for oy in range(NY) for ox in range(NX) for ok in range(NK)]
PLANE_K = [o for o in PLANE_K if o != (0, 0, 0)]
PLANE_K.sort(key=lambda o: -(min(o[0], NY - o[0]) + min(o[1], NX - o[1])))
ZS = sorted(range(1, NZ), key=lambda o: -min(o, NZ - o))


def dot_t(a, b, precision=None):
    return lax.dot_general(
        a, b, (((1,), (1,)), ((), ())), precision=precision, preferred_element_type=F32
    )


def dot(a, b, precision=None):
    return lax.dot_general(
        a, b, (((1,), (0,)), ((), ())), precision=precision, preferred_element_type=F32
    )


def eliminate(inner):
    lane = lax.broadcasted_iota(jnp.int32, (8, 128), 1)
    sub = lax.broadcasted_iota(jnp.int32, (8, 128), 0)
    tiles = []
    for v in range(RANK // 8):
        unit = jnp.where(lane == sub + (8 * v + RANK), F32(1.0), F32(0.0))
        tiles.append(jnp.where(lane < RANK, inner[8 * v : 8 * v + 8, :], unit))
    scales = [jnp.zeros((8, 128), F32) for _ in tiles]
    for j in range(RANK):
        vj, sj = j // 8, j % 8
        cols = {
            v: jnp.broadcast_to(tiles[v][:, j : j + 1], (8, 128)) for v in range(vj, RANK // 8)
        }
        row = jnp.broadcast_to(tiles[vj][sj : sj + 1, :], (8, 128))
        pivot = jnp.broadcast_to(cols[vj][sj : sj + 1, :], (8, 128))
        scales[vj] = jnp.where(sub == sj, pivot, scales[vj])
        row = row * (1.0 / pivot)
        for v in range(vj, RANK // 8):
            update = cols[v] * row
            if v == vj:
                update = jnp.where(sub > sj, update, 0.0)
            tiles[v] = tiles[v] - update
    out = [jnp.where(lane < RANK, 0.0, t * (1.0 / jnp.sqrt(s))) for t, s in zip(tiles, scales)]
    return jnp.concatenate(out, axis=0)


def kernel(
    x_hbm,
    f_ref,
    gram_out,
    nf_out,
    core_out,
    xr,
    ft,
    xcat,
    img_send,
    img_recv,
    z_send,
    z_recv,
    p_send,
    p_all,
    c_send,
    c_recv,
    lhs,
    rhs,
    g_send,
    g_recv,
    gz_send,
    gz_recv,
    gfin,
    own_sem,
    x_ss,
    x_rs,
    pair_ss,
    pair_rs,
    img_ss,
    img_rs,
    z_ss,
    z_rs,
    p_ss,
    p_rs,
    c_ss,
    c_rs,
    g_ss,
    g_rs,
    gz_ss,
    gz_rs,
):
    r = lax.axis_index("row")
    c = lax.axis_index("col")
    y, x = r // NX, r % NX
    z, k = c // NK, c % NK

    def plane(oy, ox):
        return ((y + oy) % NY) * NX + (x + ox) % NX

    def column(zz, kk):
        return zz * NK + kk

    def send(src, dst, ss, rs, row, col):
        copy = pltpu.make_async_remote_copy(
            src_ref=src,
            dst_ref=dst,
            send_sem=ss,
            recv_sem=rs,
            device_id=(row, col),
            device_id_type=MESH,
        )
        copy.start()
        return copy

    def arrival(dst, ss, rs):
        return pltpu.make_async_remote_copy(
            src_ref=dst,
            dst_ref=dst,
            send_sem=ss,
            recv_sem=rs,
            device_id=(r, c),
            device_id_type=MESH,
        )

    barrier = pltpu.get_barrier_semaphore()
    peers = 0
    for oy, ox, ok in PLANE_K:
        pl.semaphore_signal(
            barrier,
            inc=1,
            device_id=(plane(oy, ox), column(z, (k + ok) % NK)),
            device_id_type=MESH,
        )
        peers += 1
    for oz in ZS:
        for ok in range(NK):
            pl.semaphore_signal(
                barrier,
                inc=1,
                device_id=(r, column((z + oz) % NZ, (k + ok) % NK)),
                device_id_type=MESH,
            )
            peers += 1
    pl.semaphore_wait(barrier, peers)

    pending = []

    def columns_of(row):
        return pl.ds(pl.multiple_of(row * LANES, LANES), LANES)

    for i, (oy, ox) in enumerate(PLANE):
        to = plane(oy, ox)
        pending.append(
            send(x_hbm.at[:, columns_of(to)], xr.at[0, r], x_ss.at[i], x_rs.at[r], to, c)
        )
    own = pltpu.make_async_copy(x_hbm.at[:, columns_of(r)], xr.at[0, r], own_sem)
    own.start()
    ft[...] = f_ref[...].T
    own.wait()
    for oy, ox in PLANE:
        frm = plane(oy, ox)
        arrival(xr.at[0, frm], x_ss.at[0], x_rs.at[frm]).wait_recv()
    partner = column(z, 1 - k)
    pending.append(send(xr.at[0], xr.at[1], pair_ss, pair_rs, r, partner))

    rows = xr[0]
    flat = rows.reshape(MODE, LANES)
    xcat[:, 0:LANES] = rows[:, 0 : ROWS // 2, :].reshape(MODE // 2, LANES)
    xcat[:, LANES : 2 * LANES] = rows[:, ROWS // 2 :, :].reshape(MODE // 2, LANES)
    yt = dot(ft[...], flat, HIGHEST) * F32(1.0 / COLS)
    zero = jnp.zeros_like(yt)
    weights = jnp.concatenate(
        [jnp.concatenate([yt, zero], axis=1), jnp.concatenate([zero, yt], axis=1)], axis=0
    )
    term = dot_t(xcat[...], weights, HIGHEST)
    img_send[...] = term.reshape(NR, NK, 16, 128)
    me = r * NK + k
    for i, (oy, ox, ok) in enumerate(PLANE_K):
        to, kk = plane(oy, ox), (k + ok) % NK
        pending.append(
            send(
                img_send.at[to, kk],
                img_recv.at[me],
                img_ss.at[i],
                img_rs.at[me],
                to,
                column(z, kk),
            )
        )
    img_recv[me] = img_send[r, k]

    arrival(xr.at[1], pair_ss, pair_rs).wait_recv()
    for s in range(2):
        whole = xr[s].reshape(MODE, LANES)
        hi = whole.astype(BF16)
        lo = (whole - hi.astype(F32)).astype(BF16)
        rhs[:, s * LANES : (s + 1) * LANES] = hi
        rhs[:, (2 + s) * LANES : (3 + s) * LANES] = lo
        rhs[:, (4 + s) * LANES : (5 + s) * LANES] = hi
    for b in range(2 * NR):
        half = k if b < NR else 1 - k
        at = pl.ds(pl.multiple_of(32 * b + 16 * half, 16), 16)
        lhs[16 * b : 16 * b + 16, 0:256] = rhs[at, 0:256]
        lhs[16 * b : 16 * b + 16, 256:512] = rhs[at, 0:256]
        lhs[16 * b : 16 * b + 16, 512:768] = rhs[at, 256:512]
    for nb in range(4):
        part = dot_t(lhs[128 * nb : 512, :], rhs[256 * nb : 256 * nb + 256, :]) * F32(1.0 / COLS)
        for b in range(8 * nb, 2 * NR):
            to = b if b < NR else 2 * NR - 1 - b
            off = 0 if b < NR else 128 * (8 - b // 4)
            width = min(256, 128 * (b // 4 + 1) - 256 * nb)
            rows_b = part[16 * (b - 8 * nb) : 16 * (b - 8 * nb) + 16, 0:width]
            g_send[to, :, off + 256 * nb : off + 256 * nb + width] = rows_b

    for oy, ox, ok in PLANE_K:
        frm = plane(oy, ox) * NK + (k + ok) % NK
        arrival(img_recv.at[frm], img_ss.at[0], img_rs.at[frm]).wait_recv()
    total = img_recv[0]
    for s in range(1, NR * NK):
        total = total + img_recv[s]
    z_send[...] = total
    z_recv[z] = total
    for i, oz in enumerate(ZS):
        pending.append(
            send(z_send, z_recv.at[z], z_ss.at[i], z_rs.at[z], r, column((z + oz) % NZ, k))
        )
    for oz in ZS:
        frm = (z + oz) % NZ
        arrival(z_recv.at[frm], z_ss.at[0], z_rs.at[frm]).wait_recv()
    total = z_recv[0]
    for s in range(1, NZ):
        total = total + z_recv[s]
    p_send[...] = total
    p_all[me] = total
    for i, (oy, ox, ok) in enumerate(PLANE_K):
        pending.append(
            send(
                p_send,
                p_all.at[me],
                p_ss.at[i],
                p_rs.at[me],
                plane(oy, ox),
                column(z, (k + ok) % NK),
            )
        )

    for i, (oy, ox) in enumerate(PLANE):
        to = plane(oy, ox)
        pending.append(send(g_send.at[to], g_recv.at[r], g_ss.at[i], g_rs.at[r], to, c))
    g_recv[r] = g_send[r]

    for oy, ox, ok in PLANE_K:
        frm = plane(oy, ox) * NK + (k + ok) % NK
        arrival(p_all.at[frm], p_ss.at[0], p_rs.at[frm]).wait_recv()

    image = p_all[...].reshape(MODE // 2, 128)
    image_t = image.T
    inner2 = dot(image_t, image, HIGHEST)
    products = dot(image_t, xcat[...], HIGHEST)
    inner = (inner2[0:RANK, :] + pltpu.roll(inner2[RANK:, :], RANK, 1)) * F32(1.0 / MODE)
    product = products[0:RANK, 0:LANES] + products[RANK:, LANES:]
    inv_high = eliminate(inner)
    inv_low = pltpu.roll(inv_high, RANK, 1)
    core = dot(inv_low[:, 0:RANK], product, HIGHEST) * F32(1.0 / math.sqrt(MODE))
    c_send[...] = core.reshape(NR, RANK // NR, LANES)
    for i, (oy, ox) in enumerate(PLANE):
        to = plane(oy, ox)
        pending.append(send(c_send.at[to], c_recv.at[r], c_ss.at[i], c_rs.at[r], to, c))
    c_recv[r] = c_send[r]
    top = dot_t(image, inv_low, HIGHEST).reshape(NR, ROWS // 2, RANK)
    bottom = dot_t(image, inv_high, HIGHEST).reshape(NR, ROWS // 2, RANK)
    nf_out[...] = jnp.concatenate([top, bottom], axis=1).reshape(MODE, RANK)

    for oy, ox in PLANE:
        frm = plane(oy, ox)
        arrival(g_recv.at[frm], g_ss.at[0], g_rs.at[frm]).wait_recv()
    total = g_recv[0]
    for s in range(1, NR):
        total = total + g_recv[s]
    low_width = 128 * (r // 4 + 1)
    lane = lax.broadcasted_iota(jnp.int32, (2, GW), 1)
    for t in range(8):
        pair = jnp.where(lane < low_width, total[2 * t : 2 * t + 2], total[14 - 2 * t : 16 - 2 * t])
        gz_send[t] = pair
    for t in range(8):
        zz, kk = 4 * k + t // 2, t % 2
        mine = jnp.logical_and(zz == z, kk == k)

        @pl.when(jnp.logical_not(mine))
        def _():
            send(gz_send.at[t], gz_recv.at[z], gz_ss.at[t], gz_rs.at[z], r, column(zz, kk))

        @pl.when(mine)
        def _():
            gz_recv[z] = gz_send[t]

    for oy, ox in PLANE:
        frm = plane(oy, ox)
        arrival(c_recv.at[frm], c_ss.at[0], c_rs.at[frm]).wait_recv()
    for s in range(NR):
        core_out[:, LANES * s : LANES * (s + 1)] = c_recv[s]

    from_core = z // 4
    for s in range(NZ):

        @pl.when(jnp.logical_not(jnp.logical_and(s == z, from_core == k)))
        def _():
            arrival(gz_recv.at[s], gz_ss.at[0], gz_rs.at[s]).wait_recv()

    total = gz_recv[0]
    for s in range(1, NZ):
        total = total + gz_recv[s]
    gfin[...] = jnp.zeros_like(gfin)
    gfin[:, 0:GW] = total
    owner = r * (NZ * NK) + c
    row_id = lax.broadcasted_iota(jnp.int32, (2, MODE), 0)
    col_id = lax.broadcasted_iota(jnp.int32, (2, MODE), 1)
    low = gfin[:, 0:MODE]
    high = gfin[:, pl.ds(pl.multiple_of(low_width, 128), MODE)]
    gram_out[0:2, :] = jnp.where(col_id <= 2 * owner + row_id, low, 0.0)
    gram_out[2:4, :] = jnp.where(col_id <= MODE - 2 - 2 * owner + row_id, high, 0.0)

    for copy in pending:
        copy.wait_send()
    for t in range(8):
        zz, kk = 4 * k + t // 2, t % 2

        @pl.when(jnp.logical_not(jnp.logical_and(zz == z, kk == k)))
        def _():
            arrival(gz_send.at[t], gz_ss.at[t], gz_rs.at[0]).wait_send()


def body(unfolding, factor):
    dma = pltpu.SemaphoreType.DMA
    vmem = pl.BlockSpec(memory_space=pltpu.VMEM)
    return pl.pallas_call(
        kernel,
        out_shape=(
            jax.ShapeDtypeStruct((4, MODE), F32),
            jax.ShapeDtypeStruct((MODE, RANK), F32),
            jax.ShapeDtypeStruct((RANK // NR, LANES * NR), F32),
        ),
        in_specs=[pl.BlockSpec(memory_space=pl.ANY), vmem],
        out_specs=(vmem, vmem, vmem),
        scratch_shapes=[
            pltpu.VMEM((2, NR, ROWS, LANES), F32),
            pltpu.VMEM((RANK, MODE), F32),
            pltpu.VMEM((MODE // 2, 2 * LANES), F32),
            pltpu.VMEM((NR, NK, 16, 128), F32),
            pltpu.VMEM((NR * NK, 16, 128), F32),
            pltpu.VMEM((16, 128), F32),
            pltpu.VMEM((NZ, 16, 128), F32),
            pltpu.VMEM((16, 128), F32),
            pltpu.VMEM((NR * NK, 16, 128), F32),
            pltpu.VMEM((NR, RANK // NR, LANES), F32),
            pltpu.VMEM((NR, RANK // NR, LANES), F32),
            pltpu.VMEM((MODE // 2, 6 * LANES), BF16),
            pltpu.VMEM((MODE, 6 * LANES), BF16),
            pltpu.VMEM((NR, 16, GW), F32),
            pltpu.VMEM((NR, 16, GW), F32),
            pltpu.VMEM((8, 2, GW), F32),
            pltpu.VMEM((NZ, 2, GW), F32),
            pltpu.VMEM((2, 1536), F32),
            dma,
            dma((NR - 1,)),
            dma((NR,)),
            dma,
            dma,
            dma((NR * NK - 1,)),
            dma((NR * NK,)),
            dma((NZ - 1,)),
            dma((NZ,)),
            dma((NR * NK - 1,)),
            dma((NR * NK,)),
            dma((NR - 1,)),
            dma((NR,)),
            dma((NR - 1,)),
            dma((NR,)),
            dma((8,)),
            dma((NZ,)),
        ],
        compiler_params=pltpu.CompilerParams(collective_id=0, has_side_effects=True),
        name="tucker_update",
    )(unfolding, factor)


def solution(mesh):
    in_specs = (P("row", "col"), P())
    out_specs = (P(("row", "col"), None), P(), P("row", "col"))
    return jax.shard_map(body, mesh=mesh, in_specs=in_specs, out_specs=out_specs, check_vma=False)
```

```python
import functools
import math

import jax
import jax.numpy as jnp
from jax import lax
from jax.experimental import pallas as pl
from jax.experimental.pallas import tpu as pltpu
from jax.sharding import PartitionSpec as P

F32 = jnp.float32
BF16 = jnp.bfloat16
HIGHEST = lax.Precision.HIGHEST
MESH = pl.DeviceIdType.MESH

NY, NX, NZ, NK = 4, 4, 8, 2
NR = NY * NX
MODE, RANK, COLS = 1024, 64, 32768
ROWS = MODE // NR
LANES = 128
GW = 1152

PLANE = [(oy, ox) for oy in range(NY) for ox in range(NX) if (oy, ox) != (0, 0)]
PLANE.sort(key=lambda o: -(min(o[0], NY - o[0]) + min(o[1], NX - o[1])))
PLANE_K = [(oy, ox, ok) for oy in range(NY) for ox in range(NX) for ok in range(NK)]
PLANE_K = [o for o in PLANE_K if o != (0, 0, 0)]
PLANE_K.sort(key=lambda o: -(min(o[0], NY - o[0]) + min(o[1], NX - o[1])))
ZS = sorted(range(1, NZ), key=lambda o: -min(o, NZ - o))


def dot_t(a, b, precision=None):
    return lax.dot_general(
        a, b, (((1,), (1,)), ((), ())), precision=precision, preferred_element_type=F32
    )


def dot(a, b, precision=None):
    return lax.dot_general(
        a, b, (((1,), (0,)), ((), ())), precision=precision, preferred_element_type=F32
    )


def eliminate(inner):
    lane = lax.broadcasted_iota(jnp.int32, (8, 128), 1)
    sub = lax.broadcasted_iota(jnp.int32, (8, 128), 0)
    tiles = []
    for v in range(RANK // 8):
        unit = jnp.where(lane == sub + (8 * v + RANK), F32(1.0), F32(0.0))
        tiles.append(jnp.where(lane < RANK, inner[8 * v : 8 * v + 8, :], unit))
    scales = [jnp.zeros((8, 128), F32) for _ in tiles]
    for j in range(RANK):
        vj, sj = j // 8, j % 8
        cols = {
            v: jnp.broadcast_to(tiles[v][:, j : j + 1], (8, 128)) for v in range(vj, RANK // 8)
        }
        row = jnp.broadcast_to(tiles[vj][sj : sj + 1, :], (8, 128))
        pivot = jnp.broadcast_to(cols[vj][sj : sj + 1, :], (8, 128))
        scales[vj] = jnp.where(sub == sj, pivot, scales[vj])
        row = row * (1.0 / pivot)
        for v in range(vj, RANK // 8):
            update = cols[v] * row
            if v == vj:
                update = jnp.where(sub > sj, update, 0.0)
            tiles[v] = tiles[v] - update
    out = [jnp.where(lane < RANK, 0.0, t * (1.0 / jnp.sqrt(s))) for t, s in zip(tiles, scales)]
    return jnp.concatenate(out, axis=0)


def kernel(
    x_hbm,
    ft,
    gram_out,
    nf_out,
    core_out,
    xr,
    xcat,
    img_send,
    img_recv,
    z_send,
    z_recv,
    p_send,
    p_all,
    c_send,
    c_recv,
    lhs,
    rhs,
    g_send,
    g_recv,
    gz_send,
    gz_recv,
    gfin,
    own_sem,
    x_ss,
    x_rs,
    pair_ss,
    pair_rs,
    img_ss,
    img_rs,
    z_ss,
    z_rs,
    p_ss,
    p_rs,
    c_ss,
    c_rs,
    g_ss,
    g_rs,
    gz_ss,
    gz_rs,
):
    r = lax.axis_index("row")
    c = lax.axis_index("col")
    y, x = r // NX, r % NX
    z, k = c // NK, c % NK

    def plane(oy, ox):
        return ((y + oy) % NY) * NX + (x + ox) % NX

    def column(zz, kk):
        return zz * NK + kk

    def send(src, dst, ss, rs, row, col):
        copy = pltpu.make_async_remote_copy(
            src_ref=src,
            dst_ref=dst,
            send_sem=ss,
            recv_sem=rs,
            device_id=(row, col),
            device_id_type=MESH,
        )
        copy.start()
        return copy

    def arrival(dst, ss, rs):
        return pltpu.make_async_remote_copy(
            src_ref=dst,
            dst_ref=dst,
            send_sem=ss,
            recv_sem=rs,
            device_id=(r, c),
            device_id_type=MESH,
        )

    barrier = pltpu.get_barrier_semaphore()
    peers = 0
    for oy, ox, ok in PLANE_K:
        pl.semaphore_signal(
            barrier,
            inc=1,
            device_id=(plane(oy, ox), column(z, (k + ok) % NK)),
            device_id_type=MESH,
        )
        peers += 1
    for oz in ZS:
        for ok in range(NK):
            pl.semaphore_signal(
                barrier,
                inc=1,
                device_id=(r, column((z + oz) % NZ, (k + ok) % NK)),
                device_id_type=MESH,
            )
            peers += 1
    pl.semaphore_wait(barrier, peers)

    pending = []

    def columns_of(row):
        return pl.ds(pl.multiple_of(row * LANES, LANES), LANES)

    for i, (oy, ox) in enumerate(PLANE):
        to = plane(oy, ox)
        pending.append(
            send(x_hbm.at[:, columns_of(to)], xr.at[0, r], x_ss.at[i], x_rs.at[r], to, c)
        )
    own = pltpu.make_async_copy(x_hbm.at[:, columns_of(r)], xr.at[0, r], own_sem)
    own.start()
    own.wait()
    for oy, ox in PLANE:
        frm = plane(oy, ox)
        arrival(xr.at[0, frm], x_ss.at[0], x_rs.at[frm]).wait_recv()
    partner = column(z, 1 - k)
    pending.append(send(xr.at[0], xr.at[1], pair_ss, pair_rs, r, partner))

    flat = xr[0].reshape(MODE, LANES)
    xcat[:, 0:LANES] = flat[0 : MODE // 2]
    xcat[:, LANES : 2 * LANES] = flat[MODE // 2 :]
    yt = dot(ft[...], flat, HIGHEST) * F32(1.0 / COLS)
    zero = jnp.zeros_like(yt)
    weights = jnp.concatenate(
        [jnp.concatenate([yt, zero], axis=1), jnp.concatenate([zero, yt], axis=1)], axis=0
    )
    term = dot_t(xcat[...], weights, HIGHEST)
    img_send[...] = term.reshape(NR, NK, 16, 128)
    me = r * NK + k
    for i, (oy, ox, ok) in enumerate(PLANE_K):
        to, kk = plane(oy, ox), (k + ok) % NK
        pending.append(
            send(
                img_send.at[to, kk],
                img_recv.at[me],
                img_ss.at[i],
                img_rs.at[me],
                to,
                column(z, kk),
            )
        )
    img_recv[me] = img_send[r, k]

    arrival(xr.at[1], pair_ss, pair_rs).wait_recv()
    for s in range(2):
        whole = xr[s].reshape(MODE, LANES)
        hi = whole.astype(BF16)
        lo = (whole - hi.astype(F32)).astype(BF16)
        rhs[:, s * LANES : (s + 1) * LANES] = hi
        rhs[:, (2 + s) * LANES : (3 + s) * LANES] = lo
        rhs[:, (4 + s) * LANES : (5 + s) * LANES] = hi
    for b in range(2 * NR):
        half = k if b < NR else 1 - k
        at = pl.ds(pl.multiple_of(32 * b + 16 * half, 16), 16)
        lhs[16 * b : 16 * b + 16, 0:256] = rhs[at, 0:256]
        lhs[16 * b : 16 * b + 16, 256:512] = rhs[at, 0:256]
        lhs[16 * b : 16 * b + 16, 512:768] = rhs[at, 256:512]
    for nb in range(4):
        part = dot_t(lhs[128 * nb : 512, :], rhs[256 * nb : 256 * nb + 256, :]) * F32(1.0 / COLS)
        for b in range(8 * nb, 2 * NR):
            to = b if b < NR else 2 * NR - 1 - b
            off = 0 if b < NR else 128 * (8 - b // 4)
            width = min(256, 128 * (b // 4 + 1) - 256 * nb)
            rows_b = part[16 * (b - 8 * nb) : 16 * (b - 8 * nb) + 16, 0:width]
            g_send[to, :, off + 256 * nb : off + 256 * nb + width] = rows_b

    for oy, ox, ok in PLANE_K:
        frm = plane(oy, ox) * NK + (k + ok) % NK
        arrival(img_recv.at[frm], img_ss.at[0], img_rs.at[frm]).wait_recv()
    total = img_recv[0]
    for s in range(1, NR * NK):
        total = total + img_recv[s]
    z_send[...] = total
    z_recv[z] = total
    for i, oz in enumerate(ZS):
        pending.append(
            send(z_send, z_recv.at[z], z_ss.at[i], z_rs.at[z], r, column((z + oz) % NZ, k))
        )
    for oz in ZS:
        frm = (z + oz) % NZ
        arrival(z_recv.at[frm], z_ss.at[0], z_rs.at[frm]).wait_recv()
    total = z_recv[0]
    for s in range(1, NZ):
        total = total + z_recv[s]
    p_send[...] = total
    p_all[me] = total
    for i, (oy, ox, ok) in enumerate(PLANE_K):
        pending.append(
            send(
                p_send,
                p_all.at[me],
                p_ss.at[i],
                p_rs.at[me],
                plane(oy, ox),
                column(z, (k + ok) % NK),
            )
        )

    for i, (oy, ox) in enumerate(PLANE):
        to = plane(oy, ox)
        pending.append(send(g_send.at[to], g_recv.at[r], g_ss.at[i], g_rs.at[r], to, c))
    g_recv[r] = g_send[r]

    for oy, ox, ok in PLANE_K:
        frm = plane(oy, ox) * NK + (k + ok) % NK
        arrival(p_all.at[frm], p_ss.at[0], p_rs.at[frm]).wait_recv()

    image = p_all[...].reshape(MODE // 2, 128)
    image_t = image.T
    inner2 = dot(image_t, image, HIGHEST)
    products = dot(image_t, xcat[...], HIGHEST)
    inner = (inner2[0:RANK, :] + pltpu.roll(inner2[RANK:, :], RANK, 1)) * F32(1.0 / MODE)
    product = products[0:RANK, 0:LANES] + products[RANK:, LANES:]
    inv_high = eliminate(inner)
    inv_low = pltpu.roll(inv_high, RANK, 1)
    core = dot(inv_low[:, 0:RANK], product, HIGHEST) * F32(1.0 / math.sqrt(MODE))
    c_send[...] = core.reshape(NR, RANK // NR, LANES)
    for i, (oy, ox) in enumerate(PLANE):
        to = plane(oy, ox)
        pending.append(send(c_send.at[to], c_recv.at[r], c_ss.at[i], c_rs.at[r], to, c))
    c_recv[r] = c_send[r]
    nf_out[:, 0 : MODE // 2] = dot_t(inv_low, image, HIGHEST)
    nf_out[:, MODE // 2 :] = dot_t(inv_high, image, HIGHEST)

    for oy, ox in PLANE:
        frm = plane(oy, ox)
        arrival(g_recv.at[frm], g_ss.at[0], g_rs.at[frm]).wait_recv()
    total = g_recv[0]
    for s in range(1, NR):
        total = total + g_recv[s]
    low_width = 128 * (r // 4 + 1)
    lane = lax.broadcasted_iota(jnp.int32, (2, GW), 1)
    for t in range(8):
        pair = jnp.where(lane < low_width, total[2 * t : 2 * t + 2], total[14 - 2 * t : 16 - 2 * t])
        gz_send[t] = pair
    for t in range(8):
        zz, kk = 4 * k + t // 2, t % 2
        mine = jnp.logical_and(zz == z, kk == k)

        @pl.when(jnp.logical_not(mine))
        def _():
            send(gz_send.at[t], gz_recv.at[z], gz_ss.at[t], gz_rs.at[z], r, column(zz, kk))

        @pl.when(mine)
        def _():
            gz_recv[z] = gz_send[t]

    for oy, ox in PLANE:
        frm = plane(oy, ox)
        arrival(c_recv.at[frm], c_ss.at[0], c_rs.at[frm]).wait_recv()
    for s in range(NR):
        core_out[:, LANES * s : LANES * (s + 1)] = c_recv[s]

    from_core = z // 4
    for s in range(NZ):

        @pl.when(jnp.logical_not(jnp.logical_and(s == z, from_core == k)))
        def _():
            arrival(gz_recv.at[s], gz_ss.at[0], gz_rs.at[s]).wait_recv()

    total = gz_recv[0]
    for s in range(1, NZ):
        total = total + gz_recv[s]
    gfin[...] = jnp.zeros_like(gfin)
    gfin[:, 0:GW] = total
    owner = r * (NZ * NK) + c
    row_id = lax.broadcasted_iota(jnp.int32, (2, MODE), 0)
    col_id = lax.broadcasted_iota(jnp.int32, (2, MODE), 1)
    low = gfin[:, 0:MODE]
    high = gfin[:, pl.ds(pl.multiple_of(low_width, 128), MODE)]
    gram_out[0:2, :] = jnp.where(col_id <= 2 * owner + row_id, low, 0.0)
    gram_out[2:4, :] = jnp.where(col_id <= MODE - 2 - 2 * owner + row_id, high, 0.0)

    for copy in pending:
        copy.wait_send()
    for t in range(8):
        zz, kk = 4 * k + t // 2, t % 2

        @pl.when(jnp.logical_not(jnp.logical_and(zz == z, kk == k)))
        def _():
            arrival(gz_send.at[t], gz_ss.at[t], gz_rs.at[0]).wait_send()


def body(unfolding, factor):
    dma = pltpu.SemaphoreType.DMA
    vmem = pl.BlockSpec(memory_space=pltpu.VMEM)
    gram_lower, new_factor_t, core = pl.pallas_call(
        kernel,
        out_shape=(
            jax.ShapeDtypeStruct((4, MODE), F32),
            jax.ShapeDtypeStruct((RANK, MODE), F32),
            jax.ShapeDtypeStruct((RANK // NR, LANES * NR), F32),
        ),
        in_specs=[pl.BlockSpec(memory_space=pl.ANY), vmem],
        out_specs=(vmem, vmem, vmem),
        scratch_shapes=[
            pltpu.VMEM((2, NR, ROWS, LANES), F32),
            pltpu.VMEM((MODE // 2, 2 * LANES), F32),
            pltpu.VMEM((NR, NK, 16, 128), F32),
            pltpu.VMEM((NR * NK, 16, 128), F32),
            pltpu.VMEM((16, 128), F32),
            pltpu.VMEM((NZ, 16, 128), F32),
            pltpu.VMEM((16, 128), F32),
            pltpu.VMEM((NR * NK, 16, 128), F32),
            pltpu.VMEM((NR, RANK // NR, LANES), F32),
            pltpu.VMEM((NR, RANK // NR, LANES), F32),
            pltpu.VMEM((MODE // 2, 6 * LANES), BF16),
            pltpu.VMEM((MODE, 6 * LANES), BF16),
            pltpu.VMEM((NR, 16, GW), F32),
            pltpu.VMEM((NR, 16, GW), F32),
            pltpu.VMEM((8, 2, GW), F32),
            pltpu.VMEM((NZ, 2, GW), F32),
            pltpu.VMEM((2, 1536), F32),
            dma,
            dma((NR - 1,)),
            dma((NR,)),
            dma,
            dma,
            dma((NR * NK - 1,)),
            dma((NR * NK,)),
            dma((NZ - 1,)),
            dma((NZ,)),
            dma((NR * NK - 1,)),
            dma((NR * NK,)),
            dma((NR - 1,)),
            dma((NR,)),
            dma((NR - 1,)),
            dma((NR,)),
            dma((8,)),
            dma((NZ,)),
        ],
        compiler_params=pltpu.CompilerParams(collective_id=0, has_side_effects=True),
        name="tucker_update",
    )(unfolding, factor.T)
    return gram_lower, new_factor_t.T, core


def solution(mesh):
    in_specs = (P("row", "col"), P())
    out_specs = (P(("row", "col"), None), P(), P("row", "col"))
    return jax.shard_map(body, mesh=mesh, in_specs=in_specs, out_specs=out_specs, check_vma=False)
```

```python
import functools
import math

import jax
import jax.numpy as jnp
from jax import lax
from jax.experimental import pallas as pl
from jax.experimental.pallas import tpu as pltpu
from jax.sharding import PartitionSpec as P

F32 = jnp.float32
BF16 = jnp.bfloat16
HIGHEST = lax.Precision.HIGHEST
MESH = pl.DeviceIdType.MESH

NY, NX, NZ, NK = 4, 4, 8, 2
NR = NY * NX
MODE, RANK, COLS = 1024, 64, 32768
ROWS = MODE // NR
LANES = 128
GW = 1152

PLANE = [(oy, ox) for oy in range(NY) for ox in range(NX) if (oy, ox) != (0, 0)]
PLANE.sort(key=lambda o: -(min(o[0], NY - o[0]) + min(o[1], NX - o[1])))
PLANE_K = [(oy, ox, ok) for oy in range(NY) for ox in range(NX) for ok in range(NK)]
PLANE_K = [o for o in PLANE_K if o != (0, 0, 0)]
PLANE_K.sort(key=lambda o: -(min(o[0], NY - o[0]) + min(o[1], NX - o[1])))
OFFSETS = (2, 1, 3)
ZS = sorted(range(1, NZ), key=lambda o: -min(o, NZ - o))


def dot_t(a, b, precision=None):
    return lax.dot_general(
        a, b, (((1,), (1,)), ((), ())), precision=precision, preferred_element_type=F32
    )


def dot(a, b, precision=None):
    return lax.dot_general(
        a, b, (((1,), (0,)), ((), ())), precision=precision, preferred_element_type=F32
    )


def eliminate(inner):
    lane = lax.broadcasted_iota(jnp.int32, (8, 128), 1)
    sub = lax.broadcasted_iota(jnp.int32, (8, 128), 0)
    tiles = []
    for v in range(RANK // 8):
        unit = jnp.where(lane == sub + (8 * v + RANK), F32(1.0), F32(0.0))
        tiles.append(jnp.where(lane < RANK, inner[8 * v : 8 * v + 8, :], unit))

    def over_lanes(tile, j):
        return jnp.broadcast_to(tile[:, j : j + 1], (8, 128))

    def over_rows(tile, i):
        return jnp.broadcast_to(tile[i : i + 1, :], (8, 128))

    for v in range(RANK // 8):
        panel = tiles[v]
        spread = [over_lanes(panel, 8 * v + j) for j in range(8)]
        scale = jnp.ones((8, 128), F32)
        rows, links = [], []
        for s in range(8):
            pivot = over_rows(spread[s], s)
            inverse = 1.0 / pivot
            scale = jnp.where(sub == s, pivot, scale)
            row = over_rows(panel, s) * inverse
            link = [over_rows(spread[j], s) * inverse for j in range(s + 1, 8)]
            factor = jnp.where(sub > s, spread[s], 0.0)
            for j in range(s + 1, 8):
                spread[j] = spread[j] - factor * link[j - s - 1]
            panel = panel - factor * row
            rows.append(row)
            links.append(link)
        tiles[v] = panel * (1.0 / jnp.sqrt(scale))
        for w in range(v + 1, RANK // 8):
            spread = [over_lanes(tiles[w], 8 * v + j) for j in range(8)]
            for s in range(8):
                for j in range(s + 1, 8):
                    spread[j] = spread[j] - spread[s] * links[s][j - s - 1]
                tiles[w] = tiles[w] - spread[s] * rows[s]
    return jnp.concatenate([jnp.where(lane < RANK, 0.0, t) for t in tiles], axis=0)


def kernel(
    x_hbm,
    ft,
    gram_out,
    nf_out,
    core_out,
    xr,
    xcat,
    img_send,
    img_recv,
    z_send,
    z_recv,
    p_send,
    p_all,
    c_send,
    c_recv,
    lhs,
    rhs,
    ga,
    ga_recv,
    gb,
    gb_recv,
    gz_send,
    gz_recv,
    gfin,
    own_sem,
    x_ss,
    x_rs,
    pair_ss,
    pair_rs,
    img_ss,
    img_rs,
    z_ss,
    z_rs,
    p_ss,
    p_rs,
    c_ss,
    c_rs,
    ga_ss,
    ga_rs,
    gb_ss,
    gb_rs,
    gz_ss,
    gz_rs,
):
    r = lax.axis_index("row")
    c = lax.axis_index("col")
    y, x = r // NX, r % NX
    z, k = c // NK, c % NK

    def plane(oy, ox):
        return ((y + oy) % NY) * NX + (x + ox) % NX

    def column(zz, kk):
        return zz * NK + kk

    def send(src, dst, ss, rs, row, col):
        copy = pltpu.make_async_remote_copy(
            src_ref=src,
            dst_ref=dst,
            send_sem=ss,
            recv_sem=rs,
            device_id=(row, col),
            device_id_type=MESH,
        )
        copy.start()
        return copy

    def arrival(dst, ss, rs):
        return pltpu.make_async_remote_copy(
            src_ref=dst,
            dst_ref=dst,
            send_sem=ss,
            recv_sem=rs,
            device_id=(r, c),
            device_id_type=MESH,
        )

    barrier = pltpu.get_barrier_semaphore()
    peers = 0
    for oy, ox, ok in PLANE_K:
        pl.semaphore_signal(
            barrier,
            inc=1,
            device_id=(plane(oy, ox), column(z, (k + ok) % NK)),
            device_id_type=MESH,
        )
        peers += 1
    for oz in ZS:
        for ok in range(NK):
            pl.semaphore_signal(
                barrier,
                inc=1,
                device_id=(r, column((z + oz) % NZ, (k + ok) % NK)),
                device_id_type=MESH,
            )
            peers += 1
    pl.semaphore_wait(barrier, peers)

    pending = []

    def columns_of(row):
        return pl.ds(pl.multiple_of(row * LANES, LANES), LANES)

    for i, (oy, ox) in enumerate(PLANE):
        to = plane(oy, ox)
        pending.append(
            send(x_hbm.at[:, columns_of(to)], xr.at[0, r], x_ss.at[i], x_rs.at[r], to, c)
        )
    own = pltpu.make_async_copy(x_hbm.at[:, columns_of(r)], xr.at[0, r], own_sem)
    own.start()
    own.wait()
    for oy, ox in PLANE:
        frm = plane(oy, ox)
        arrival(xr.at[0, frm], x_ss.at[0], x_rs.at[frm]).wait_recv()
    partner = column(z, 1 - k)
    pending.append(send(xr.at[0], xr.at[1], pair_ss, pair_rs, r, partner))

    flat = xr[0].reshape(MODE, LANES)
    xcat[:, 0:LANES] = flat[0 : MODE // 2]
    xcat[:, LANES : 2 * LANES] = flat[MODE // 2 :]
    yt = dot(ft[...], flat, HIGHEST) * F32(1.0 / COLS)
    zero = jnp.zeros_like(yt)
    weights = jnp.concatenate(
        [jnp.concatenate([yt, zero], axis=1), jnp.concatenate([zero, yt], axis=1)], axis=0
    )
    term = dot_t(xcat[...], weights, HIGHEST)
    img_send[...] = term.reshape(NR, NK, 16, 128)
    me = r * NK + k
    for i, (oy, ox, ok) in enumerate(PLANE_K):
        to, kk = plane(oy, ox), (k + ok) % NK
        pending.append(
            send(
                img_send.at[to, kk],
                img_recv.at[me],
                img_ss.at[i],
                img_rs.at[me],
                to,
                column(z, kk),
            )
        )
    img_recv[me] = img_send[r, k]

    arrival(xr.at[1], pair_ss, pair_rs).wait_recv()
    for s in range(2):
        whole = xr[s].reshape(MODE, LANES)
        hi = whole.astype(BF16)
        lo = (whole - hi.astype(F32)).astype(BF16)
        rhs[:, s * LANES : (s + 1) * LANES] = hi
        rhs[:, (2 + s) * LANES : (3 + s) * LANES] = lo
        rhs[:, (4 + s) * LANES : (5 + s) * LANES] = hi
    for b in range(2 * NR):
        half = k if b < NR else 1 - k
        at = pl.ds(pl.multiple_of(32 * b + 16 * half, 16), 16)
        lhs[16 * b : 16 * b + 16, 0:256] = rhs[at, 0:256]
        lhs[16 * b : 16 * b + 16, 256:512] = rhs[at, 0:256]
        lhs[16 * b : 16 * b + 16, 512:768] = rhs[at, 256:512]
    for nb in range(4):
        part = dot_t(lhs[128 * nb : 512, :], rhs[256 * nb : 256 * nb + 256, :]) * F32(1.0 / COLS)
        for b in range(8 * nb, 2 * NR):
            to = b if b < NR else 2 * NR - 1 - b
            off = 0 if b < NR else 128 * (8 - b // 4)
            width = min(256, 128 * (b // 4 + 1) - 256 * nb)
            rows_b = part[16 * (b - 8 * nb) : 16 * (b - 8 * nb) + 16, 0:width]
            at = pl.ds(off + 256 * nb, width)
            ga[0, to % NX, to // NX, :, at] = rows_b[0:8]
            ga[1, to // NX, to % NX, :, at] = rows_b[8:16]
    for i in range(3):
        xx, yy = (x + OFFSETS[i]) % NX, (y + OFFSETS[i]) % NY
        pending.append(
            send(ga.at[0, xx], ga_recv.at[0, x], ga_ss.at[0, i], ga_rs.at[0, x], y * NX + xx, c)
        )
        pending.append(
            send(ga.at[1, yy], ga_recv.at[1, y], ga_ss.at[1, i], ga_rs.at[1, y], yy * NX + x, c)
        )

    for oy, ox, ok in PLANE_K:
        frm = plane(oy, ox) * NK + (k + ok) % NK
        arrival(img_recv.at[frm], img_ss.at[0], img_rs.at[frm]).wait_recv()
    total = img_recv[0]
    for s in range(1, NR * NK):
        total = total + img_recv[s]
    z_send[...] = total
    z_recv[z] = total
    for i, oz in enumerate(ZS):
        pending.append(
            send(z_send, z_recv.at[z], z_ss.at[i], z_rs.at[z], r, column((z + oz) % NZ, k))
        )
    for oz in ZS:
        frm = (z + oz) % NZ
        arrival(z_recv.at[frm], z_ss.at[0], z_rs.at[frm]).wait_recv()
    total = z_recv[0]
    for s in range(1, NZ):
        total = total + z_recv[s]
    p_send[...] = total
    p_all[me] = total
    for i, (oy, ox, ok) in enumerate(PLANE_K):
        pending.append(
            send(
                p_send,
                p_all.at[me],
                p_ss.at[i],
                p_rs.at[me],
                plane(oy, ox),
                column(z, (k + ok) % NK),
            )
        )

    for h, at in ((0, x), (1, y)):
        total = ga[h, at]
        for i in range(3):
            frm = (at + OFFSETS[i]) % 4
            arrival(ga_recv.at[h, frm], ga_ss.at[h, 0], ga_rs.at[h, frm]).wait_recv()
            total = total + ga_recv[h, frm]
        gb[h] = total
    for i in range(3):
        xx, yy = (x + OFFSETS[i]) % NX, (y + OFFSETS[i]) % NY
        pending.append(
            send(gb.at[0, yy], gb_recv.at[0, y], gb_ss.at[0, i], gb_rs.at[0, y], yy * NX + x, c)
        )
        pending.append(
            send(gb.at[1, xx], gb_recv.at[1, x], gb_ss.at[1, i], gb_rs.at[1, x], y * NX + xx, c)
        )

    for oy, ox, ok in PLANE_K:
        frm = plane(oy, ox) * NK + (k + ok) % NK
        arrival(p_all.at[frm], p_ss.at[0], p_rs.at[frm]).wait_recv()

    image = p_all[...].reshape(MODE // 2, 128)
    image_t = image.T
    inner2 = dot(image_t, image, HIGHEST)
    products = dot(image_t, xcat[...], HIGHEST)
    inner = (inner2[0:RANK, :] + pltpu.roll(inner2[RANK:, :], RANK, 1)) * F32(1.0 / MODE)
    product = products[0:RANK, 0:LANES] + products[RANK:, LANES:]
    halves = []
    for h, at in ((0, y), (1, x)):
        total = gb[h, at]
        for i in range(3):
            frm = (at + OFFSETS[i]) % 4
            arrival(gb_recv.at[h, frm], gb_ss.at[h, 0], gb_rs.at[h, frm]).wait_recv()
            total = total + gb_recv[h, frm]
        halves.append(total)
    total = jnp.concatenate(halves, axis=0)
    low_width = 128 * (r // 4 + 1)
    lane = lax.broadcasted_iota(jnp.int32, (2, GW), 1)
    for t in range(8):
        pair = jnp.where(lane < low_width, total[2 * t : 2 * t + 2], total[14 - 2 * t : 16 - 2 * t])
        gz_send[t] = pair
    for t in range(8):
        zz, kk = 4 * k + t // 2, t % 2
        mine = jnp.logical_and(zz == z, kk == k)

        @pl.when(jnp.logical_not(mine))
        def _():
            send(gz_send.at[t], gz_recv.at[z], gz_ss.at[t], gz_rs.at[z], r, column(zz, kk))

        @pl.when(mine)
        def _():
            gz_recv[z] = gz_send[t]

    inv_high = eliminate(inner)
    inv_low = pltpu.roll(inv_high, RANK, 1)
    core = dot(inv_low[:, 0:RANK], product, HIGHEST) * F32(1.0 / math.sqrt(MODE))
    c_send[...] = core.reshape(NR, RANK // NR, LANES)
    for i, (oy, ox) in enumerate(PLANE):
        to = plane(oy, ox)
        pending.append(send(c_send.at[to], c_recv.at[r], c_ss.at[i], c_rs.at[r], to, c))
    c_recv[r] = c_send[r]
    nf_out[:, 0 : MODE // 2] = dot_t(inv_low, image, HIGHEST)
    nf_out[:, MODE // 2 :] = dot_t(inv_high, image, HIGHEST)

    for oy, ox in PLANE:
        frm = plane(oy, ox)
        arrival(c_recv.at[frm], c_ss.at[0], c_rs.at[frm]).wait_recv()
    for s in range(NR):
        core_out[:, LANES * s : LANES * (s + 1)] = c_recv[s]

    from_core = z // 4
    for s in range(NZ):

        @pl.when(jnp.logical_not(jnp.logical_and(s == z, from_core == k)))
        def _():
            arrival(gz_recv.at[s], gz_ss.at[0], gz_rs.at[s]).wait_recv()

    total = gz_recv[0]
    for s in range(1, NZ):
        total = total + gz_recv[s]
    gfin[...] = jnp.zeros_like(gfin)
    gfin[:, 0:GW] = total
    owner = r * (NZ * NK) + c
    row_id = lax.broadcasted_iota(jnp.int32, (2, MODE), 0)
    col_id = lax.broadcasted_iota(jnp.int32, (2, MODE), 1)
    low = gfin[:, 0:MODE]
    high = gfin[:, pl.ds(pl.multiple_of(low_width, 128), MODE)]
    gram_out[0:2, :] = jnp.where(col_id <= 2 * owner + row_id, low, 0.0)
    gram_out[2:4, :] = jnp.where(col_id <= MODE - 2 - 2 * owner + row_id, high, 0.0)

    for copy in pending:
        copy.wait_send()
    for t in range(8):
        zz, kk = 4 * k + t // 2, t % 2

        @pl.when(jnp.logical_not(jnp.logical_and(zz == z, kk == k)))
        def _():
            arrival(gz_send.at[t], gz_ss.at[t], gz_rs.at[0]).wait_send()


def body(unfolding, factor):
    dma = pltpu.SemaphoreType.DMA
    vmem = pl.BlockSpec(memory_space=pltpu.VMEM)
    gram_lower, new_factor_t, core = pl.pallas_call(
        kernel,
        out_shape=(
            jax.ShapeDtypeStruct((4, MODE), F32),
            jax.ShapeDtypeStruct((RANK, MODE), F32),
            jax.ShapeDtypeStruct((RANK // NR, LANES * NR), F32),
        ),
        in_specs=[pl.BlockSpec(memory_space=pl.ANY), vmem],
        out_specs=(vmem, vmem, vmem),
        scratch_shapes=[
            pltpu.VMEM((2, NR, ROWS, LANES), F32),
            pltpu.VMEM((MODE // 2, 2 * LANES), F32),
            pltpu.VMEM((NR, NK, 16, 128), F32),
            pltpu.VMEM((NR * NK, 16, 128), F32),
            pltpu.VMEM((16, 128), F32),
            pltpu.VMEM((NZ, 16, 128), F32),
            pltpu.VMEM((16, 128), F32),
            pltpu.VMEM((NR * NK, 16, 128), F32),
            pltpu.VMEM((NR, RANK // NR, LANES), F32),
            pltpu.VMEM((NR, RANK // NR, LANES), F32),
            pltpu.VMEM((MODE // 2, 6 * LANES), BF16),
            pltpu.VMEM((MODE, 6 * LANES), BF16),
            pltpu.VMEM((2, 4, 4, 8, GW), F32),
            pltpu.VMEM((2, 4, 4, 8, GW), F32),
            pltpu.VMEM((2, 4, 8, GW), F32),
            pltpu.VMEM((2, 4, 8, GW), F32),
            pltpu.VMEM((8, 2, GW), F32),
            pltpu.VMEM((NZ, 2, GW), F32),
            pltpu.VMEM((2, 1536), F32),
            dma,
            dma((NR - 1,)),
            dma((NR,)),
            dma,
            dma,
            dma((NR * NK - 1,)),
            dma((NR * NK,)),
            dma((NZ - 1,)),
            dma((NZ,)),
            dma((NR * NK - 1,)),
            dma((NR * NK,)),
            dma((NR - 1,)),
            dma((NR,)),
            dma((2, 3)),
            dma((2, 4)),
            dma((2, 3)),
            dma((2, 4)),
            dma((8,)),
            dma((NZ,)),
        ],
        compiler_params=pltpu.CompilerParams(
            collective_id=0, has_side_effects=True, vmem_limit_bytes=32 * 1024 * 1024
        ),
        name="tucker_update",
    )(unfolding, factor.T)
    return gram_lower, new_factor_t.T, core


def solution(mesh):
    in_specs = (P("row", "col"), P())
    out_specs = (P(("row", "col"), None), P(), P("row", "col"))
    return jax.shard_map(body, mesh=mesh, in_specs=in_specs, out_specs=out_specs, check_vma=False)
```

```python
import functools
import math

import jax
import jax.numpy as jnp
from jax import lax
from jax.experimental import pallas as pl
from jax.experimental.pallas import tpu as pltpu
from jax.sharding import PartitionSpec as P

F32 = jnp.float32
BF16 = jnp.bfloat16
HIGHEST = lax.Precision.HIGHEST
MESH = pl.DeviceIdType.MESH

NY, NX, NZ, NK = 4, 4, 8, 2
NR = NY * NX
MODE, RANK, COLS = 1024, 64, 32768
ROWS = MODE // NR
LANES = 128
GW = 1152

PLANE = [(oy, ox) for oy in range(NY) for ox in range(NX) if (oy, ox) != (0, 0)]
PLANE.sort(key=lambda o: -(min(o[0], NY - o[0]) + min(o[1], NX - o[1])))
PLANE_K = [(oy, ox, ok) for oy in range(NY) for ox in range(NX) for ok in range(NK)]
PLANE_K = [o for o in PLANE_K if o != (0, 0, 0)]
PLANE_K.sort(key=lambda o: -(min(o[0], NY - o[0]) + min(o[1], NX - o[1])))
OFFSETS = (2, 1, 3)
ZS = sorted(range(1, NZ), key=lambda o: -min(o, NZ - o))


def dot_t(a, b, precision=None):
    return lax.dot_general(
        a, b, (((1,), (1,)), ((), ())), precision=precision, preferred_element_type=F32
    )


def dot(a, b, precision=None):
    return lax.dot_general(
        a, b, (((1,), (0,)), ((), ())), precision=precision, preferred_element_type=F32
    )


def split(a):
    hi = a.astype(BF16)
    return hi, (a - hi.astype(F32)).astype(BF16)


def dot3(a, b):
    (ah, al), (bh, bl) = split(a), split(b)
    return dot(jnp.concatenate([ah, ah, al], axis=1), jnp.concatenate([bh, bl, bh], axis=0))


def dot3_t(a, b):
    (ah, al), (bh, bl) = split(a), split(b)
    return dot_t(jnp.concatenate([ah, ah, al], axis=1), jnp.concatenate([bh, bl, bh], axis=1))


def eliminate(inner):
    lane = lax.broadcasted_iota(jnp.int32, (8, 128), 1)
    sub = lax.broadcasted_iota(jnp.int32, (8, 128), 0)
    tiles = []
    for v in range(RANK // 8):
        unit = jnp.where(lane == sub + (8 * v + RANK), F32(1.0), F32(0.0))
        tiles.append(jnp.where(lane < RANK, inner[8 * v : 8 * v + 8, :], unit))

    def over_lanes(tile, j):
        return jnp.broadcast_to(tile[:, j : j + 1], (8, 128))

    def over_rows(tile, i):
        return jnp.broadcast_to(tile[i : i + 1, :], (8, 128))

    for v in range(RANK // 8):
        panel = tiles[v]
        spread = [over_lanes(panel, 8 * v + j) for j in range(8)]
        scale = jnp.ones((8, 128), F32)
        rows, links = [], []
        for s in range(8):
            pivot = over_rows(spread[s], s)
            inverse = 1.0 / pivot
            scale = jnp.where(sub == s, pivot, scale)
            row = over_rows(panel, s) * inverse
            link = [over_rows(spread[j], s) * inverse for j in range(s + 1, 8)]
            factor = jnp.where(sub > s, spread[s], 0.0)
            for j in range(s + 1, 8):
                spread[j] = spread[j] - factor * link[j - s - 1]
            panel = panel - factor * row
            rows.append(row)
            links.append(link)
        tiles[v] = panel * (1.0 / jnp.sqrt(scale))
        for w in range(v + 1, RANK // 8):
            spread = [over_lanes(tiles[w], 8 * v + j) for j in range(8)]
            for s in range(8):
                for j in range(s + 1, 8):
                    spread[j] = spread[j] - spread[s] * links[s][j - s - 1]
                tiles[w] = tiles[w] - spread[s] * rows[s]
    return jnp.concatenate([jnp.where(lane < RANK, 0.0, t) for t in tiles], axis=0)


def kernel(
    x_hbm,
    ft_hbm,
    gram_out,
    nf_out,
    core_out,
    xr,
    ft,
    xcat,
    img_send,
    img_recv,
    z_send,
    z_recv,
    p_send,
    p_all,
    c_send,
    c_recv,
    lhs,
    rhs,
    ga,
    ga_recv,
    gb,
    gb_recv,
    gz_send,
    gz_recv,
    gfin,
    own_sem,
    ft_sem,
    x_ss,
    x_rs,
    pair_ss,
    pair_rs,
    img_ss,
    img_rs,
    z_ss,
    z_rs,
    p_ss,
    p_rs,
    c_ss,
    c_rs,
    ga_ss,
    ga_rs,
    gb_ss,
    gb_rs,
    gz_ss,
    gz_rs,
):
    r = lax.axis_index("row")
    c = lax.axis_index("col")
    y, x = r // NX, r % NX
    z, k = c // NK, c % NK

    def plane(oy, ox):
        return ((y + oy) % NY) * NX + (x + ox) % NX

    def column(zz, kk):
        return zz * NK + kk

    def send(src, dst, ss, rs, row, col):
        copy = pltpu.make_async_remote_copy(
            src_ref=src,
            dst_ref=dst,
            send_sem=ss,
            recv_sem=rs,
            device_id=(row, col),
            device_id_type=MESH,
        )
        copy.start()
        return copy

    def arrival(dst, ss, rs):
        return pltpu.make_async_remote_copy(
            src_ref=dst,
            dst_ref=dst,
            send_sem=ss,
            recv_sem=rs,
            device_id=(r, c),
            device_id_type=MESH,
        )

    barrier = pltpu.get_barrier_semaphore()
    peers = 0
    for oz in ZS:
        for ok in range(NK):
            pl.semaphore_signal(
                barrier,
                inc=1,
                device_id=(r, column((z + oz) % NZ, (k + ok) % NK)),
                device_id_type=MESH,
            )
            peers += 1
    for oy, ox, ok in PLANE_K:
        pl.semaphore_signal(
            barrier,
            inc=1,
            device_id=(plane(oy, ox), column(z, (k + ok) % NK)),
            device_id_type=MESH,
        )
        peers += 1
    factor_copy = pltpu.make_async_copy(ft_hbm, ft, ft_sem)
    factor_copy.start()
    pl.semaphore_wait(barrier, peers)

    pending = []

    def columns_of(row):
        return pl.ds(pl.multiple_of(row * LANES, LANES), LANES)

    for i, (oy, ox) in enumerate(PLANE):
        to = plane(oy, ox)
        pending.append(
            send(x_hbm.at[:, columns_of(to)], xr.at[0, r], x_ss.at[i], x_rs.at[r], to, c)
        )
    own = pltpu.make_async_copy(x_hbm.at[:, columns_of(r)], xr.at[0, r], own_sem)
    own.start()
    own.wait()
    factor_copy.wait()
    for oy, ox in PLANE:
        frm = plane(oy, ox)
        arrival(xr.at[0, frm], x_ss.at[0], x_rs.at[frm]).wait_recv()
    partner = column(z, 1 - k)
    pending.append(send(xr.at[0], xr.at[1], pair_ss, pair_rs, r, partner))

    flat = xr[0].reshape(MODE, LANES)
    xcat[:, 0:LANES] = flat[0 : MODE // 2]
    xcat[:, LANES : 2 * LANES] = flat[MODE // 2 :]
    yt = dot3(ft[...], flat) * F32(1.0 / COLS)
    zero = jnp.zeros_like(yt)
    weights = jnp.concatenate(
        [jnp.concatenate([yt, zero], axis=1), jnp.concatenate([zero, yt], axis=1)], axis=0
    )
    term = dot3_t(xcat[...], weights)
    img_send[...] = term.reshape(NR, NK, 16, 128)
    me = r * NK + k
    for i, (oy, ox, ok) in enumerate(PLANE_K):
        to, kk = plane(oy, ox), (k + ok) % NK
        pending.append(
            send(
                img_send.at[to, kk],
                img_recv.at[me],
                img_ss.at[i],
                img_rs.at[me],
                to,
                column(z, kk),
            )
        )
    img_recv[me] = img_send[r, k]

    arrival(xr.at[1], pair_ss, pair_rs).wait_recv()
    for s in range(2):
        whole = xr[s].reshape(MODE, LANES)
        hi = whole.astype(BF16)
        lo = (whole - hi.astype(F32)).astype(BF16)
        rhs[:, s * LANES : (s + 1) * LANES] = hi
        rhs[:, (2 + s) * LANES : (3 + s) * LANES] = lo
        rhs[:, (4 + s) * LANES : (5 + s) * LANES] = hi
    for b in range(2 * NR):
        half = k if b < NR else 1 - k
        at = pl.ds(pl.multiple_of(32 * b + 16 * half, 16), 16)
        lhs[16 * b : 16 * b + 16, 0:256] = rhs[at, 0:256]
        lhs[16 * b : 16 * b + 16, 256:512] = rhs[at, 0:256]
        lhs[16 * b : 16 * b + 16, 512:768] = rhs[at, 256:512]
    for nb in range(4):
        part = dot_t(lhs[128 * nb : 512, :], rhs[256 * nb : 256 * nb + 256, :]) * F32(1.0 / COLS)
        for b in range(8 * nb, 2 * NR):
            to = b if b < NR else 2 * NR - 1 - b
            off = 0 if b < NR else 128 * (8 - b // 4)
            width = min(256, 128 * (b // 4 + 1) - 256 * nb)
            rows_b = part[16 * (b - 8 * nb) : 16 * (b - 8 * nb) + 16, 0:width]
            at = pl.ds(off + 256 * nb, width)
            ga[0, to % NX, to // NX, :, at] = rows_b[0:8]
            ga[1, to // NX, to % NX, :, at] = rows_b[8:16]
    for i in range(3):
        xx, yy = (x + OFFSETS[i]) % NX, (y + OFFSETS[i]) % NY
        pending.append(
            send(ga.at[0, xx], ga_recv.at[0, x], ga_ss.at[0, i], ga_rs.at[0, x], y * NX + xx, c)
        )
        pending.append(
            send(ga.at[1, yy], ga_recv.at[1, y], ga_ss.at[1, i], ga_rs.at[1, y], yy * NX + x, c)
        )

    for oy, ox, ok in PLANE_K:
        frm = plane(oy, ox) * NK + (k + ok) % NK
        arrival(img_recv.at[frm], img_ss.at[0], img_rs.at[frm]).wait_recv()
    total = img_recv[0]
    for s in range(1, NR * NK):
        total = total + img_recv[s]
    z_send[...] = total
    z_recv[z] = total
    for i, oz in enumerate(ZS):
        pending.append(
            send(z_send, z_recv.at[z], z_ss.at[i], z_rs.at[z], r, column((z + oz) % NZ, k))
        )
    for oz in ZS:
        frm = (z + oz) % NZ
        arrival(z_recv.at[frm], z_ss.at[0], z_rs.at[frm]).wait_recv()
    total = z_recv[0]
    for s in range(1, NZ):
        total = total + z_recv[s]
    p_send[...] = total
    p_all[me] = total
    for i, (oy, ox, ok) in enumerate(PLANE_K):
        pending.append(
            send(
                p_send,
                p_all.at[me],
                p_ss.at[i],
                p_rs.at[me],
                plane(oy, ox),
                column(z, (k + ok) % NK),
            )
        )

    for h, at in ((0, x), (1, y)):
        total = ga[h, at]
        for i in range(3):
            frm = (at + OFFSETS[i]) % 4
            arrival(ga_recv.at[h, frm], ga_ss.at[h, 0], ga_rs.at[h, frm]).wait_recv()
            total = total + ga_recv[h, frm]
        gb[h] = total
    for i in range(3):
        xx, yy = (x + OFFSETS[i]) % NX, (y + OFFSETS[i]) % NY
        pending.append(
            send(gb.at[0, yy], gb_recv.at[0, y], gb_ss.at[0, i], gb_rs.at[0, y], yy * NX + x, c)
        )
        pending.append(
            send(gb.at[1, xx], gb_recv.at[1, x], gb_ss.at[1, i], gb_rs.at[1, x], y * NX + xx, c)
        )

    for oy, ox, ok in PLANE_K:
        frm = plane(oy, ox) * NK + (k + ok) % NK
        arrival(p_all.at[frm], p_ss.at[0], p_rs.at[frm]).wait_recv()

    image = p_all[...].reshape(MODE // 2, 128)
    image_t = image.T
    inner2 = dot3(image_t, image)
    products = dot3(image_t, xcat[...])
    inner = (inner2[0:RANK, :] + pltpu.roll(inner2[RANK:, :], RANK, 1)) * F32(1.0 / MODE)
    product = products[0:RANK, 0:LANES] + products[RANK:, LANES:]
    inv_high = eliminate(inner)
    inv_low = pltpu.roll(inv_high, RANK, 1)
    core = dot(inv_low[:, 0:RANK], product, HIGHEST) * F32(1.0 / math.sqrt(MODE))
    c_send[...] = core.reshape(NR, RANK // NR, LANES)
    for i, (oy, ox) in enumerate(PLANE):
        to = plane(oy, ox)
        pending.append(send(c_send.at[to], c_recv.at[r], c_ss.at[i], c_rs.at[r], to, c))
    c_recv[r] = c_send[r]
    nf_out[:, 0 : MODE // 2] = dot3_t(inv_low, image)
    nf_out[:, MODE // 2 :] = dot3_t(inv_high, image)

    halves = []
    for h, at in ((0, y), (1, x)):
        total = gb[h, at]
        for i in range(3):
            frm = (at + OFFSETS[i]) % 4
            arrival(gb_recv.at[h, frm], gb_ss.at[h, 0], gb_rs.at[h, frm]).wait_recv()
            total = total + gb_recv[h, frm]
        halves.append(total)
    total = jnp.concatenate(halves, axis=0)
    low_width = 128 * (r // 4 + 1)
    lane = lax.broadcasted_iota(jnp.int32, (2, GW), 1)
    for t in range(8):
        pair = jnp.where(lane < low_width, total[2 * t : 2 * t + 2], total[14 - 2 * t : 16 - 2 * t])
        gz_send[t] = pair
    for t in range(8):
        zz, kk = 4 * k + t // 2, t % 2
        mine = jnp.logical_and(zz == z, kk == k)

        @pl.when(jnp.logical_not(mine))
        def _():
            send(gz_send.at[t], gz_recv.at[z], gz_ss.at[t], gz_rs.at[z], r, column(zz, kk))

        @pl.when(mine)
        def _():
            gz_recv[z] = gz_send[t]

    for oy, ox in PLANE:
        frm = plane(oy, ox)
        arrival(c_recv.at[frm], c_ss.at[0], c_rs.at[frm]).wait_recv()
    for s in range(NR):
        core_out[:, LANES * s : LANES * (s + 1)] = c_recv[s]

    from_core = z // 4
    for s in range(NZ):

        @pl.when(jnp.logical_not(jnp.logical_and(s == z, from_core == k)))
        def _():
            arrival(gz_recv.at[s], gz_ss.at[0], gz_rs.at[s]).wait_recv()

    total = gz_recv[0]
    for s in range(1, NZ):
        total = total + gz_recv[s]
    gfin[...] = jnp.zeros_like(gfin)
    gfin[:, 0:GW] = total
    owner = r * (NZ * NK) + c
    row_id = lax.broadcasted_iota(jnp.int32, (2, MODE), 0)
    col_id = lax.broadcasted_iota(jnp.int32, (2, MODE), 1)
    low = gfin[:, 0:MODE]
    high = gfin[:, pl.ds(pl.multiple_of(low_width, 128), MODE)]
    gram_out[0:2, :] = jnp.where(col_id <= 2 * owner + row_id, low, 0.0)
    gram_out[2:4, :] = jnp.where(col_id <= MODE - 2 - 2 * owner + row_id, high, 0.0)

    for copy in pending:
        copy.wait_send()
    for t in range(8):
        zz, kk = 4 * k + t // 2, t % 2

        @pl.when(jnp.logical_not(jnp.logical_and(zz == z, kk == k)))
        def _():
            arrival(gz_send.at[t], gz_ss.at[t], gz_rs.at[0]).wait_send()


def finish(gram_in, nf_in, core_in, gram_out, nf_out, core_out, sems):
    copies = []
    for i, (src, dst) in enumerate(((nf_in, nf_out), (core_in, core_out), (gram_in, gram_out))):
        copies.append(pltpu.make_async_copy(src, dst, sems.at[i]))
        copies[-1].start()
    for copy in copies:
        copy.wait()


def body(unfolding, factor):
    dma = pltpu.SemaphoreType.DMA
    hbm = functools.partial(pltpu.with_memory_space_constraint, memory_space=pltpu.HBM)
    vmem = pl.BlockSpec(memory_space=pltpu.VMEM)
    gram_lower, new_factor_t, core = pl.pallas_call(
        kernel,
        out_shape=(
            jax.ShapeDtypeStruct((4, MODE), F32),
            jax.ShapeDtypeStruct((RANK, MODE), F32),
            jax.ShapeDtypeStruct((RANK // NR, LANES * NR), F32),
        ),
        in_specs=[pl.BlockSpec(memory_space=pl.ANY)] * 2,
        out_specs=(vmem, vmem, vmem),
        scratch_shapes=[
            pltpu.VMEM((2, NR, ROWS, LANES), F32),
            pltpu.VMEM((RANK, MODE), F32),
            pltpu.VMEM((MODE // 2, 2 * LANES), F32),
            pltpu.VMEM((NR, NK, 16, 128), F32),
            pltpu.VMEM((NR * NK, 16, 128), F32),
            pltpu.VMEM((16, 128), F32),
            pltpu.VMEM((NZ, 16, 128), F32),
            pltpu.VMEM((16, 128), F32),
            pltpu.VMEM((NR * NK, 16, 128), F32),
            pltpu.VMEM((NR, RANK // NR, LANES), F32),
            pltpu.VMEM((NR, RANK // NR, LANES), F32),
            pltpu.VMEM((MODE // 2, 6 * LANES), BF16),
            pltpu.VMEM((MODE, 6 * LANES), BF16),
            pltpu.VMEM((2, 4, 4, 8, GW), F32),
            pltpu.VMEM((2, 4, 4, 8, GW), F32),
            pltpu.VMEM((2, 4, 8, GW), F32),
            pltpu.VMEM((2, 4, 8, GW), F32),
            pltpu.VMEM((8, 2, GW), F32),
            pltpu.VMEM((NZ, 2, GW), F32),
            pltpu.VMEM((2, 1536), F32),
            dma,
            dma,
            dma((NR - 1,)),
            dma((NR,)),
            dma,
            dma,
            dma((NR * NK - 1,)),
            dma((NR * NK,)),
            dma((NZ - 1,)),
            dma((NZ,)),
            dma((NR * NK - 1,)),
            dma((NR * NK,)),
            dma((NR - 1,)),
            dma((NR,)),
            dma((2, 3)),
            dma((2, 4)),
            dma((2, 3)),
            dma((2, 4)),
            dma((8,)),
            dma((NZ,)),
        ],
        compiler_params=pltpu.CompilerParams(
            collective_id=0, has_side_effects=True, vmem_limit_bytes=32 * 1024 * 1024
        ),
        name="tucker_update",
    )(hbm(unfolding), hbm(factor.T))
    anywhere = pl.BlockSpec(memory_space=pl.ANY)
    gram_lower, new_factor_t, core = pl.pallas_call(
        finish,
        out_shape=(
            jax.ShapeDtypeStruct((4, MODE), F32),
            jax.ShapeDtypeStruct((RANK, MODE), F32),
            jax.ShapeDtypeStruct((RANK // NR, LANES * NR), F32),
        ),
        in_specs=[anywhere, anywhere, anywhere],
        out_specs=(anywhere, anywhere, anywhere),
        scratch_shapes=[pltpu.SemaphoreType.DMA((3,))],
        compiler_params=pltpu.CompilerParams(vmem_limit_bytes=1024 * 1024),
        name="write_results",
    )(gram_lower, new_factor_t, core)
    return gram_lower, new_factor_t.T, core


def solution(mesh):
    in_specs = (P("row", "col"), P())
    out_specs = (P(("row", "col"), None), P(), P("row", "col"))
    return jax.shard_map(body, mesh=mesh, in_specs=in_specs, out_specs=out_specs, check_vma=False)
```

```python
import functools
import math

import jax
import jax.numpy as jnp
from jax import lax
from jax.experimental import pallas as pl
from jax.experimental.pallas import tpu as pltpu
from jax.sharding import PartitionSpec as P

F32 = jnp.float32
BF16 = jnp.bfloat16
HIGHEST = lax.Precision.HIGHEST
MESH = pl.DeviceIdType.MESH

NY, NX, NZ, NK = 4, 4, 8, 2
NR = NY * NX
MODE, RANK, COLS = 1024, 64, 32768
ROWS = MODE // NR
LANES = 128
GW = 1152

PLANE = [(oy, ox) for oy in range(NY) for ox in range(NX) if (oy, ox) != (0, 0)]
PLANE.sort(key=lambda o: -(min(o[0], NY - o[0]) + min(o[1], NX - o[1])))
PLANE_K = [(oy, ox, ok) for oy in range(NY) for ox in range(NX) for ok in range(NK)]
PLANE_K = [o for o in PLANE_K if o != (0, 0, 0)]
PLANE_K.sort(key=lambda o: -(min(o[0], NY - o[0]) + min(o[1], NX - o[1])))
OFFSETS = (2, 1, 3)
ZS = sorted(range(1, NZ), key=lambda o: -min(o, NZ - o))


def dot_t(a, b, precision=None):
    return lax.dot_general(
        a, b, (((1,), (1,)), ((), ())), precision=precision, preferred_element_type=F32
    )


def dot(a, b, precision=None):
    return lax.dot_general(
        a, b, (((1,), (0,)), ((), ())), precision=precision, preferred_element_type=F32
    )


def split(a):
    hi = a.astype(BF16)
    return hi, (a - hi.astype(F32)).astype(BF16)


def dot3(a, b):
    (ah, al), (bh, bl) = split(a), split(b)
    return dot(jnp.concatenate([ah, ah, al], axis=1), jnp.concatenate([bh, bl, bh], axis=0))


def dot3_t(a, b):
    (ah, al), (bh, bl) = split(a), split(b)
    return dot_t(jnp.concatenate([ah, ah, al], axis=1), jnp.concatenate([bh, bl, bh], axis=1))


def eliminate(inner):
    lane = lax.broadcasted_iota(jnp.int32, (8, 128), 1)
    sub = lax.broadcasted_iota(jnp.int32, (8, 128), 0)
    tiles = []
    for v in range(RANK // 8):
        unit = jnp.where(lane == sub + (8 * v + RANK), F32(1.0), F32(0.0))
        tiles.append(jnp.where(lane < RANK, inner[8 * v : 8 * v + 8, :], unit))

    def over_lanes(tile, j):
        return jnp.broadcast_to(tile[:, j : j + 1], (8, 128))

    def over_rows(tile, i):
        return jnp.broadcast_to(tile[i : i + 1, :], (8, 128))

    for v in range(RANK // 8):
        panel = tiles[v]
        spread = [over_lanes(panel, 8 * v + j) for j in range(8)]
        scale = jnp.ones((8, 128), F32)
        rows, links = [], []
        for s in range(8):
            pivot = over_rows(spread[s], s)
            inverse = 1.0 / pivot
            scale = jnp.where(sub == s, pivot, scale)
            row = over_rows(panel, s) * inverse
            link = [over_rows(spread[j], s) * inverse for j in range(s + 1, 8)]
            factor = jnp.where(sub > s, spread[s], 0.0)
            for j in range(s + 1, 8):
                spread[j] = spread[j] - factor * link[j - s - 1]
            panel = panel - factor * row
            rows.append(row)
            links.append(link)
        tiles[v] = panel * (1.0 / jnp.sqrt(scale))
        for w in range(v + 1, RANK // 8):
            spread = [over_lanes(tiles[w], 8 * v + j) for j in range(8)]
            for s in range(8):
                for j in range(s + 1, 8):
                    spread[j] = spread[j] - spread[s] * links[s][j - s - 1]
                tiles[w] = tiles[w] - spread[s] * rows[s]
    return jnp.concatenate([jnp.where(lane < RANK, 0.0, t) for t in tiles], axis=0)


def kernel(
    x_hbm,
    ft_hbm,
    gram_out,
    nf_out,
    core_out,
    xr,
    ft,
    xcat,
    img_send,
    img_recv,
    z_send,
    z_recv,
    p_send,
    p_all,
    c_send,
    c_recv,
    lhs,
    rhs,
    ga,
    ga_recv,
    gb,
    gb_recv,
    gz_send,
    gz_recv,
    gfin,
    own_sem,
    ft_sem,
    x_ss,
    x_rs,
    pair_ss,
    pair_rs,
    img_ss,
    img_rs,
    z_ss,
    z_rs,
    p_ss,
    p_rs,
    c_ss,
    c_rs,
    ga_ss,
    ga_rs,
    gb_ss,
    gb_rs,
    gz_ss,
    gz_rs,
):
    r = lax.axis_index("row")
    c = lax.axis_index("col")
    y, x = r // NX, r % NX
    z, k = c // NK, c % NK

    def plane(oy, ox):
        return ((y + oy) % NY) * NX + (x + ox) % NX

    def column(zz, kk):
        return zz * NK + kk

    def send(src, dst, ss, rs, row, col):
        copy = pltpu.make_async_remote_copy(
            src_ref=src,
            dst_ref=dst,
            send_sem=ss,
            recv_sem=rs,
            device_id=(row, col),
            device_id_type=MESH,
        )
        copy.start()
        return copy

    def arrival(dst, ss, rs):
        return pltpu.make_async_remote_copy(
            src_ref=dst,
            dst_ref=dst,
            send_sem=ss,
            recv_sem=rs,
            device_id=(r, c),
            device_id_type=MESH,
        )

    barrier = pltpu.get_barrier_semaphore()
    peers = 0
    for oz in ZS:
        for ok in range(NK):
            pl.semaphore_signal(
                barrier,
                inc=1,
                device_id=(r, column((z + oz) % NZ, (k + ok) % NK)),
                device_id_type=MESH,
            )
            peers += 1
    for oy, ox, ok in PLANE_K:
        pl.semaphore_signal(
            barrier,
            inc=1,
            device_id=(plane(oy, ox), column(z, (k + ok) % NK)),
            device_id_type=MESH,
        )
        peers += 1
    factor_copy = pltpu.make_async_copy(ft_hbm, ft, ft_sem)
    factor_copy.start()
    pl.semaphore_wait(barrier, peers)

    pending = []

    def columns_of(row):
        return pl.ds(pl.multiple_of(row * LANES, LANES), LANES)

    for i, (oy, ox) in enumerate(PLANE):
        to = plane(oy, ox)
        pending.append(
            send(x_hbm.at[:, columns_of(to)], xr.at[0, r], x_ss.at[i], x_rs.at[r], to, c)
        )
    own = pltpu.make_async_copy(x_hbm.at[:, columns_of(r)], xr.at[0, r], own_sem)
    own.start()
    own.wait()
    factor_copy.wait()
    for oy, ox in PLANE:
        frm = plane(oy, ox)
        arrival(xr.at[0, frm], x_ss.at[0], x_rs.at[frm]).wait_recv()
    partner = column(z, 1 - k)
    pending.append(send(xr.at[0], xr.at[1], pair_ss, pair_rs, r, partner))

    flat = xr[0].reshape(MODE, LANES)
    xcat[:, 0:LANES] = flat[0 : MODE // 2]
    xcat[:, LANES : 2 * LANES] = flat[MODE // 2 :]
    yt = dot3(ft[...], flat) * F32(1.0 / COLS)
    zero = jnp.zeros_like(yt)
    weights = jnp.concatenate(
        [jnp.concatenate([yt, zero], axis=1), jnp.concatenate([zero, yt], axis=1)], axis=0
    )
    term = dot3_t(xcat[...], weights)
    img_send[...] = term.reshape(NR, NK, 16, 128)
    me = r * NK + k
    for i, (oy, ox, ok) in enumerate(PLANE_K):
        to, kk = plane(oy, ox), (k + ok) % NK
        pending.append(
            send(
                img_send.at[to, kk],
                img_recv.at[me],
                img_ss.at[i],
                img_rs.at[me],
                to,
                column(z, kk),
            )
        )
    img_recv[me] = img_send[r, k]

    arrival(xr.at[1], pair_ss, pair_rs).wait_recv()
    for s in range(2):
        whole = xr[s].reshape(MODE, LANES)
        hi = whole.astype(BF16)
        lo = (whole - hi.astype(F32)).astype(BF16)
        rhs[:, s * LANES : (s + 1) * LANES] = hi
        rhs[:, (2 + s) * LANES : (3 + s) * LANES] = lo
        rhs[:, (4 + s) * LANES : (5 + s) * LANES] = hi
    for b in range(2 * NR):
        half = k if b < NR else 1 - k
        at = pl.ds(pl.multiple_of(32 * b + 16 * half, 16), 16)
        lhs[16 * b : 16 * b + 16, 0:256] = rhs[at, 0:256]
        lhs[16 * b : 16 * b + 16, 256:512] = rhs[at, 0:256]
        lhs[16 * b : 16 * b + 16, 512:768] = rhs[at, 256:512]
    at_row = lax.broadcasted_iota(jnp.int32, (256, 256), 0)
    at_col = lax.broadcasted_iota(jnp.int32, (256, 256), 1)
    mirrored = at_row - at_row % 16 + 14 - at_row % 16 + 2 * (at_row % 2)
    order = jnp.where(at_col == mirrored, F32(1.0), F32(0.0)).astype(BF16)
    lhs[256:512, 0:256] = dot(order, lhs[256:512, 0:256]).astype(BF16)
    lhs[256:512, 256:512] = lhs[256:512, 0:256]
    lhs[256:512, 512:768] = dot(order, lhs[256:512, 512:768]).astype(BF16)
    for nb in range(4):
        part = dot_t(lhs[128 * nb : 512, :], rhs[256 * nb : 256 * nb + 256, :]) * F32(1.0 / COLS)
        for b in range(8 * nb, 2 * NR):
            to = b if b < NR else 2 * NR - 1 - b
            off = 0 if b < NR else 128 * (8 - b // 4)
            width = min(256, 128 * (b // 4 + 1) - 256 * nb)
            rows_b = part[16 * (b - 8 * nb) : 16 * (b - 8 * nb) + 16, 0:width]
            at = pl.ds(off + 256 * nb, width)
            ga[0, to % NX, to // NX, :, at] = rows_b[0:8]
            ga[1, to // NX, to % NX, :, at] = rows_b[8:16]
    for i in range(3):
        xx, yy = (x + OFFSETS[i]) % NX, (y + OFFSETS[i]) % NY
        pending.append(
            send(ga.at[0, xx], ga_recv.at[0, x], ga_ss.at[0, i], ga_rs.at[0, x], y * NX + xx, c)
        )
        pending.append(
            send(ga.at[1, yy], ga_recv.at[1, y], ga_ss.at[1, i], ga_rs.at[1, y], yy * NX + x, c)
        )

    for oy, ox, ok in PLANE_K:
        frm = plane(oy, ox) * NK + (k + ok) % NK
        arrival(img_recv.at[frm], img_ss.at[0], img_rs.at[frm]).wait_recv()
    total = img_recv[0]
    for s in range(1, NR * NK):
        total = total + img_recv[s]
    z_send[...] = total
    z_recv[z] = total
    for i, oz in enumerate(ZS):
        pending.append(
            send(z_send, z_recv.at[z], z_ss.at[i], z_rs.at[z], r, column((z + oz) % NZ, k))
        )
    for oz in ZS:
        frm = (z + oz) % NZ
        arrival(z_recv.at[frm], z_ss.at[0], z_rs.at[frm]).wait_recv()
    total = z_recv[0]
    for s in range(1, NZ):
        total = total + z_recv[s]
    p_send[...] = total
    p_all[me] = total
    for i, (oy, ox, ok) in enumerate(PLANE_K):
        pending.append(
            send(
                p_send,
                p_all.at[me],
                p_ss.at[i],
                p_rs.at[me],
                plane(oy, ox),
                column(z, (k + ok) % NK),
            )
        )

    for h, at in ((0, x), (1, y)):
        total = ga[h, at]
        for i in range(3):
            frm = (at + OFFSETS[i]) % 4
            arrival(ga_recv.at[h, frm], ga_ss.at[h, 0], ga_rs.at[h, frm]).wait_recv()
            total = total + ga_recv[h, frm]
        for t in range(4):
            gz_send[4 * h + t] = total[:, 2 * t : 2 * t + 2]
    for t in range(8):
        zz, kk = 4 * k + t // 2, t % 2
        mine = jnp.logical_and(zz == z, kk == k)

        @pl.when(jnp.logical_not(mine))
        def _():
            send(gz_send.at[t], gz_recv.at[z], gz_ss.at[t], gz_rs.at[z], r, column(zz, kk))

        @pl.when(mine)
        def _():
            gz_recv[z] = gz_send[t]

    for oy, ox, ok in PLANE_K:
        frm = plane(oy, ox) * NK + (k + ok) % NK
        arrival(p_all.at[frm], p_ss.at[0], p_rs.at[frm]).wait_recv()

    image = p_all[...].reshape(MODE // 2, 128)
    image_t = image.T
    inner2 = dot3(image_t, image)
    products = dot3(image_t, xcat[...])
    inner = (inner2[0:RANK, :] + pltpu.roll(inner2[RANK:, :], RANK, 1)) * F32(1.0 / MODE)
    product = products[0:RANK, 0:LANES] + products[RANK:, LANES:]
    inv_high = eliminate(inner)
    inv_low = pltpu.roll(inv_high, RANK, 1)
    core = dot(inv_low[:, 0:RANK], product, HIGHEST) * F32(1.0 / math.sqrt(MODE))
    c_send[...] = core.reshape(NR, RANK // NR, LANES)
    for i, (oy, ox) in enumerate(PLANE):
        to = plane(oy, ox)
        pending.append(send(c_send.at[to], c_recv.at[r], c_ss.at[i], c_rs.at[r], to, c))
    c_recv[r] = c_send[r]
    nf_out[:, 0 : MODE // 2] = dot3_t(inv_low, image)
    nf_out[:, MODE // 2 :] = dot3_t(inv_high, image)

    from_core = z // 4
    for s in range(NZ):

        @pl.when(jnp.logical_not(jnp.logical_and(s == z, from_core == k)))
        def _():
            arrival(gz_recv.at[s], gz_ss.at[0], gz_rs.at[s]).wait_recv()

    total = gz_recv[0]
    for s in range(1, NZ):
        total = total + gz_recv[s]
    gb[...] = total
    along_y = z % 4 < 2
    at = jnp.where(along_y, y, x)
    for i in range(3):
        to = (at + OFFSETS[i]) % 4
        row = jnp.where(along_y, to * NX + x, y * NX + to)
        pending.append(send(gb.at[to], gb_recv.at[at], gb_ss.at[i], gb_rs.at[at], row, c))

    for oy, ox in PLANE:
        frm = plane(oy, ox)
        arrival(c_recv.at[frm], c_ss.at[0], c_rs.at[frm]).wait_recv()
    for s in range(NR):
        core_out[:, LANES * s : LANES * (s + 1)] = c_recv[s]

    total = gb[at]
    for i in range(3):
        frm = (at + OFFSETS[i]) % 4
        arrival(gb_recv.at[frm], gb_ss.at[0], gb_rs.at[frm]).wait_recv()
        total = total + gb_recv[frm]
    low_width = 128 * (r // 4 + 1)
    gfin[...] = jnp.zeros_like(gfin)
    gfin[:, 0:GW] = total
    owner = r * (NZ * NK) + c
    row_id = lax.broadcasted_iota(jnp.int32, (2, MODE), 0)
    col_id = lax.broadcasted_iota(jnp.int32, (2, MODE), 1)
    low = gfin[:, 0:MODE]
    high = gfin[:, pl.ds(pl.multiple_of(low_width, 128), MODE)]
    gram_out[0:2, :] = jnp.where(col_id <= 2 * owner + row_id, low, 0.0)
    gram_out[2:4, :] = jnp.where(col_id <= MODE - 2 - 2 * owner + row_id, high, 0.0)

    for copy in pending:
        copy.wait_send()
    for t in range(8):
        zz, kk = 4 * k + t // 2, t % 2

        @pl.when(jnp.logical_not(jnp.logical_and(zz == z, kk == k)))
        def _():
            arrival(gz_send.at[t], gz_ss.at[t], gz_rs.at[0]).wait_send()


def finish(gram_in, nf_in, core_in, gram_out, nf_out, core_out, sems):
    copies = []
    for i, (src, dst) in enumerate(((nf_in, nf_out), (core_in, core_out), (gram_in, gram_out))):
        copies.append(pltpu.make_async_copy(src, dst, sems.at[i]))
        copies[-1].start()
    for copy in copies:
        copy.wait()


def body(unfolding, factor):
    dma = pltpu.SemaphoreType.DMA
    hbm = functools.partial(pltpu.with_memory_space_constraint, memory_space=pltpu.HBM)
    vmem = pl.BlockSpec(memory_space=pltpu.VMEM)
    gram_lower, new_factor_t, core = pl.pallas_call(
        kernel,
        out_shape=(
            jax.ShapeDtypeStruct((4, MODE), F32),
            jax.ShapeDtypeStruct((RANK, MODE), F32),
            jax.ShapeDtypeStruct((RANK // NR, LANES * NR), F32),
        ),
        in_specs=[pl.BlockSpec(memory_space=pl.ANY)] * 2,
        out_specs=(vmem, vmem, vmem),
        scratch_shapes=[
            pltpu.VMEM((2, NR, ROWS, LANES), F32),
            pltpu.VMEM((RANK, MODE), F32),
            pltpu.VMEM((MODE // 2, 2 * LANES), F32),
            pltpu.VMEM((NR, NK, 16, 128), F32),
            pltpu.VMEM((NR * NK, 16, 128), F32),
            pltpu.VMEM((16, 128), F32),
            pltpu.VMEM((NZ, 16, 128), F32),
            pltpu.VMEM((16, 128), F32),
            pltpu.VMEM((NR * NK, 16, 128), F32),
            pltpu.VMEM((NR, RANK // NR, LANES), F32),
            pltpu.VMEM((NR, RANK // NR, LANES), F32),
            pltpu.VMEM((MODE // 2, 6 * LANES), BF16),
            pltpu.VMEM((MODE, 6 * LANES), BF16),
            pltpu.VMEM((2, 4, 4, 8, GW), F32),
            pltpu.VMEM((2, 4, 4, 8, GW), F32),
            pltpu.VMEM((4, 2, GW), F32),
            pltpu.VMEM((4, 2, GW), F32),
            pltpu.VMEM((8, 4, 2, GW), F32),
            pltpu.VMEM((NZ, 4, 2, GW), F32),
            pltpu.VMEM((2, 1536), F32),
            dma,
            dma,
            dma((NR - 1,)),
            dma((NR,)),
            dma,
            dma,
            dma((NR * NK - 1,)),
            dma((NR * NK,)),
            dma((NZ - 1,)),
            dma((NZ,)),
            dma((NR * NK - 1,)),
            dma((NR * NK,)),
            dma((NR - 1,)),
            dma((NR,)),
            dma((2, 3)),
            dma((2, 4)),
            dma((3,)),
            dma((4,)),
            dma((8,)),
            dma((NZ,)),
        ],
        compiler_params=pltpu.CompilerParams(
            collective_id=0, has_side_effects=True, vmem_limit_bytes=32 * 1024 * 1024
        ),
        name="tucker_update",
    )(hbm(unfolding), hbm(factor.T))
    anywhere = pl.BlockSpec(memory_space=pl.ANY)
    gram_lower, new_factor_t, core = pl.pallas_call(
        finish,
        out_shape=(
            jax.ShapeDtypeStruct((4, MODE), F32),
            jax.ShapeDtypeStruct((RANK, MODE), F32),
            jax.ShapeDtypeStruct((RANK // NR, LANES * NR), F32),
        ),
        in_specs=[anywhere, anywhere, anywhere],
        out_specs=(anywhere, anywhere, anywhere),
        scratch_shapes=[pltpu.SemaphoreType.DMA((3,))],
        compiler_params=pltpu.CompilerParams(vmem_limit_bytes=1024 * 1024),
        name="write_results",
    )(gram_lower, new_factor_t, core)
    return gram_lower, new_factor_t.T, core


def solution(mesh):
    in_specs = (P("row", "col"), P())
    out_specs = (P(("row", "col"), None), P(), P("row", "col"))
    return jax.shard_map(body, mesh=mesh, in_specs=in_specs, out_specs=out_specs, check_vma=False)
```

```python
import functools
import math

import jax
import jax.numpy as jnp
from jax import lax
from jax.experimental import pallas as pl
from jax.experimental.pallas import tpu as pltpu
from jax.sharding import PartitionSpec as P

F32 = jnp.float32
BF16 = jnp.bfloat16
HIGHEST = lax.Precision.HIGHEST
MESH = pl.DeviceIdType.MESH

NY, NX, NZ, NK = 4, 4, 8, 2
NR = NY * NX
MODE, RANK, COLS = 1024, 64, 32768
ROWS = MODE // NR
LANES = 128
GW = 1152

PLANE = [(oy, ox) for oy in range(NY) for ox in range(NX) if (oy, ox) != (0, 0)]
PLANE.sort(key=lambda o: -(min(o[0], NY - o[0]) + min(o[1], NX - o[1])))
PLANE_K = [(oy, ox, ok) for oy in range(NY) for ox in range(NX) for ok in range(NK)]
PLANE_K = [o for o in PLANE_K if o != (0, 0, 0)]
PLANE_K.sort(key=lambda o: -(min(o[0], NY - o[0]) + min(o[1], NX - o[1])))
OFFSETS = (1, 3, 2)
ZS = sorted(range(1, NZ), key=lambda o: -min(o, NZ - o))


def dot_t(a, b, precision=None):
    return lax.dot_general(
        a, b, (((1,), (1,)), ((), ())), precision=precision, preferred_element_type=F32
    )


def dot(a, b, precision=None):
    return lax.dot_general(
        a, b, (((1,), (0,)), ((), ())), precision=precision, preferred_element_type=F32
    )


def split(a):
    hi = a.astype(BF16)
    return hi, (a - hi.astype(F32)).astype(BF16)


def dot3(a, b):
    (ah, al), (bh, bl) = split(a), split(b)
    return dot(jnp.concatenate([ah, ah, al], axis=1), jnp.concatenate([bh, bl, bh], axis=0))


def dot3_t(a, b):
    (ah, al), (bh, bl) = split(a), split(b)
    return dot_t(jnp.concatenate([ah, ah, al], axis=1), jnp.concatenate([bh, bl, bh], axis=1))


def eliminate(inner):
    lane = lax.broadcasted_iota(jnp.int32, (8, 128), 1)
    sub = lax.broadcasted_iota(jnp.int32, (8, 128), 0)
    tiles = []
    for v in range(RANK // 8):
        unit = jnp.where(lane == sub + (8 * v + RANK), F32(1.0), F32(0.0))
        tiles.append(jnp.where(lane < RANK, inner[8 * v : 8 * v + 8, :], unit))

    def over_lanes(tile, j):
        return jnp.broadcast_to(tile[:, j : j + 1], (8, 128))

    def over_rows(tile, i):
        return jnp.broadcast_to(tile[i : i + 1, :], (8, 128))

    for v in range(RANK // 8):
        panel = tiles[v]
        spread = [over_lanes(panel, 8 * v + j) for j in range(8)]
        scale = jnp.ones((8, 128), F32)
        rows, links = [], []
        for s in range(8):
            pivot = over_rows(spread[s], s)
            inverse = 1.0 / pivot
            scale = jnp.where(sub == s, pivot, scale)
            row = over_rows(panel, s) * inverse
            link = [over_rows(spread[j], s) * inverse for j in range(s + 1, 8)]
            factor = jnp.where(sub > s, spread[s], 0.0)
            for j in range(s + 1, 8):
                spread[j] = spread[j] - factor * link[j - s - 1]
            panel = panel - factor * row
            rows.append(row)
            links.append(link)
        tiles[v] = panel * (1.0 / jnp.sqrt(scale))
        for w in range(v + 1, RANK // 8):
            spread = [over_lanes(tiles[w], 8 * v + j) for j in range(8)]
            for s in range(8):
                for j in range(s + 1, 8):
                    spread[j] = spread[j] - spread[s] * links[s][j - s - 1]
                tiles[w] = tiles[w] - spread[s] * rows[s]
    return jnp.concatenate([jnp.where(lane < RANK, 0.0, t) for t in tiles], axis=0)


def kernel(
    x_hbm,
    ft_hbm,
    gram_out,
    nf_out,
    core_out,
    xr,
    ft,
    xcat,
    img_send,
    img_recv,
    z_send,
    z_recv,
    p_send,
    p_all,
    c_send,
    c_recv,
    lhs,
    rhs,
    ga,
    ga_recv,
    gb,
    gb_recv,
    gz_send,
    gz_recv,
    gfin,
    own_sem,
    ft_sem,
    x_ss,
    x_rs,
    pair_ss,
    pair_rs,
    img_ss,
    img_rs,
    z_ss,
    z_rs,
    p_ss,
    p_rs,
    c_ss,
    c_rs,
    ga_ss,
    ga_rs,
    gb_ss,
    gb_rs,
    gz_ss,
    gz_rs,
):
    r = lax.axis_index("row")
    c = lax.axis_index("col")
    y, x = r // NX, r % NX
    z, k = c // NK, c % NK

    def plane(oy, ox):
        return ((y + oy) % NY) * NX + (x + ox) % NX

    def column(zz, kk):
        return zz * NK + kk

    def send(src, dst, ss, rs, row, col):
        copy = pltpu.make_async_remote_copy(
            src_ref=src,
            dst_ref=dst,
            send_sem=ss,
            recv_sem=rs,
            device_id=(row, col),
            device_id_type=MESH,
        )
        copy.start()
        return copy

    def arrival(dst, ss, rs):
        return pltpu.make_async_remote_copy(
            src_ref=dst,
            dst_ref=dst,
            send_sem=ss,
            recv_sem=rs,
            device_id=(r, c),
            device_id_type=MESH,
        )

    barrier = pltpu.get_barrier_semaphore()
    peers = 0
    for oz in ZS:
        for ok in range(NK):
            pl.semaphore_signal(
                barrier,
                inc=1,
                device_id=(r, column((z + oz) % NZ, (k + ok) % NK)),
                device_id_type=MESH,
            )
            peers += 1
    for oy, ox, ok in PLANE_K:
        pl.semaphore_signal(
            barrier,
            inc=1,
            device_id=(plane(oy, ox), column(z, (k + ok) % NK)),
            device_id_type=MESH,
        )
        peers += 1
    factor_copy = pltpu.make_async_copy(ft_hbm, ft, ft_sem)
    factor_copy.start()
    pl.semaphore_wait(barrier, peers)

    pending = []

    def columns_of(row):
        return pl.ds(pl.multiple_of(row * LANES, LANES), LANES)

    for i, (oy, ox) in enumerate(PLANE):
        to = plane(oy, ox)
        pending.append(
            send(x_hbm.at[:, columns_of(to)], xr.at[0, r], x_ss.at[i], x_rs.at[r], to, c)
        )
    own = pltpu.make_async_copy(x_hbm.at[:, columns_of(r)], xr.at[0, r], own_sem)
    own.start()
    own.wait()
    factor_copy.wait()
    for oy, ox in PLANE:
        frm = plane(oy, ox)
        arrival(xr.at[0, frm], x_ss.at[0], x_rs.at[frm]).wait_recv()
    partner = column(z, 1 - k)
    pending.append(send(xr.at[0], xr.at[1], pair_ss, pair_rs, r, partner))

    flat = xr[0].reshape(MODE, LANES)
    xcat[:, 0:LANES] = flat[0 : MODE // 2]
    xcat[:, LANES : 2 * LANES] = flat[MODE // 2 :]
    yt = dot3(ft[...], flat) * F32(1.0 / COLS)
    zero = jnp.zeros_like(yt)
    weights = jnp.concatenate(
        [jnp.concatenate([yt, zero], axis=1), jnp.concatenate([zero, yt], axis=1)], axis=0
    )
    term = dot3_t(xcat[...], weights)
    img_send[...] = term.reshape(NR, NK, 16, 128)
    me = r * NK + k
    for i, (oy, ox, ok) in enumerate(PLANE_K):
        to, kk = plane(oy, ox), (k + ok) % NK
        pending.append(
            send(
                img_send.at[to, kk],
                img_recv.at[me],
                img_ss.at[i],
                img_rs.at[me],
                to,
                column(z, kk),
            )
        )
    img_recv[me] = img_send[r, k]

    arrival(xr.at[1], pair_ss, pair_rs).wait_recv()
    for s in range(2):
        whole = xr[s].reshape(MODE, LANES)
        hi = whole.astype(BF16)
        lo = (whole - hi.astype(F32)).astype(BF16)
        rhs[:, s * LANES : (s + 1) * LANES] = hi
        rhs[:, (2 + s) * LANES : (3 + s) * LANES] = lo
        rhs[:, (4 + s) * LANES : (5 + s) * LANES] = hi
    for b in range(2 * NR):
        half = k if b < NR else 1 - k
        at = pl.ds(pl.multiple_of(32 * b + 16 * half, 16), 16)
        lhs[16 * b : 16 * b + 16, 0:256] = rhs[at, 0:256]
        lhs[16 * b : 16 * b + 16, 256:512] = rhs[at, 0:256]
        lhs[16 * b : 16 * b + 16, 512:768] = rhs[at, 256:512]
    at_row = lax.broadcasted_iota(jnp.int32, (256, 256), 0)
    at_col = lax.broadcasted_iota(jnp.int32, (256, 256), 1)
    mirrored = at_row - at_row % 16 + 14 - at_row % 16 + 2 * (at_row % 2)
    order = jnp.where(at_col == mirrored, F32(1.0), F32(0.0)).astype(BF16)
    lhs[256:512, 0:256] = dot(order, lhs[256:512, 0:256]).astype(BF16)
    lhs[256:512, 256:512] = lhs[256:512, 0:256]
    lhs[256:512, 512:768] = dot(order, lhs[256:512, 512:768]).astype(BF16)
    for nb in range(4):
        part = dot_t(lhs[128 * nb : 512, :], rhs[256 * nb : 256 * nb + 256, :]) * F32(1.0 / COLS)
        for b in range(8 * nb, 2 * NR):
            to = b if b < NR else 2 * NR - 1 - b
            off = 0 if b < NR else 128 * (8 - b // 4)
            width = min(256, 128 * (b // 4 + 1) - 256 * nb)
            rows_b = part[16 * (b - 8 * nb) : 16 * (b - 8 * nb) + 16, 0:width]
            at = pl.ds(off + 256 * nb, width)
            ga[0, to % NX, to // NX, :, at] = rows_b[0:8]
            ga[1, to // NX, to % NX, :, at] = rows_b[8:16]
    for i in range(3):
        xx, yy = (x + OFFSETS[i]) % NX, (y + OFFSETS[i]) % NY
        pending.append(
            send(ga.at[0, xx], ga_recv.at[0, x], ga_ss.at[0, i], ga_rs.at[0, x], y * NX + xx, c)
        )
        pending.append(
            send(ga.at[1, yy], ga_recv.at[1, y], ga_ss.at[1, i], ga_rs.at[1, y], yy * NX + x, c)
        )

    for oy, ox, ok in PLANE_K:
        frm = plane(oy, ox) * NK + (k + ok) % NK
        arrival(img_recv.at[frm], img_ss.at[0], img_rs.at[frm]).wait_recv()
    total = img_recv[0]
    for s in range(1, NR * NK):
        total = total + img_recv[s]
    z_send[...] = total
    z_recv[z] = total
    for i, oz in enumerate(ZS):
        pending.append(
            send(z_send, z_recv.at[z], z_ss.at[i], z_rs.at[z], r, column((z + oz) % NZ, k))
        )
    for oz in ZS:
        frm = (z + oz) % NZ
        arrival(z_recv.at[frm], z_ss.at[0], z_rs.at[frm]).wait_recv()
    total = z_recv[0]
    for s in range(1, NZ):
        total = total + z_recv[s]
    p_send[...] = total
    p_all[me] = total
    for i, (oy, ox, ok) in enumerate(sorted(PLANE_K, key=lambda o: min(o[0], NY - o[0]) + min(o[1], NX - o[1]))):
        pending.append(
            send(
                p_send,
                p_all.at[me],
                p_ss.at[i],
                p_rs.at[me],
                plane(oy, ox),
                column(z, (k + ok) % NK),
            )
        )

    for h, at in ((0, x), (1, y)):
        total = ga[h, at]
        for i in range(3):
            frm = (at + OFFSETS[i]) % 4
            arrival(ga_recv.at[h, frm], ga_ss.at[h, 0], ga_rs.at[h, frm]).wait_recv()
            total = total + ga_recv[h, frm]
        for t in range(4):
            gz_send[4 * h + t] = total[:, 2 * t : 2 * t + 2]
    for t in range(8):
        zz, kk = 4 * k + t // 2, t % 2
        mine = jnp.logical_and(zz == z, kk == k)

        @pl.when(jnp.logical_not(mine))
        def _():
            send(gz_send.at[t], gz_recv.at[z], gz_ss.at[t], gz_rs.at[z], r, column(zz, kk))

        @pl.when(mine)
        def _():
            gz_recv[z] = gz_send[t]

    for oy, ox, ok in PLANE_K:
        frm = plane(oy, ox) * NK + (k + ok) % NK
        arrival(p_all.at[frm], p_ss.at[0], p_rs.at[frm]).wait_recv()

    image = p_all[...].reshape(MODE // 2, 128)
    image_t = image.T
    inner2 = dot3(image_t, image)
    products = dot3(image_t, xcat[...])
    inner = (inner2[0:RANK, :] + pltpu.roll(inner2[RANK:, :], RANK, 1)) * F32(1.0 / MODE)
    product = products[0:RANK, 0:LANES] + products[RANK:, LANES:]
    inv_high = eliminate(inner)
    inv_low = pltpu.roll(inv_high, RANK, 1)
    core = dot(inv_low[:, 0:RANK], product, HIGHEST) * F32(1.0 / math.sqrt(MODE))
    c_send[...] = core.reshape(NR, RANK // NR, LANES)
    for i, (oy, ox) in enumerate(PLANE):
        to = plane(oy, ox)
        pending.append(send(c_send.at[to], c_recv.at[r], c_ss.at[i], c_rs.at[r], to, c))
    c_recv[r] = c_send[r]

    from_core = z // 4
    for s in range(NZ):

        @pl.when(jnp.logical_not(jnp.logical_and(s == z, from_core == k)))
        def _():
            arrival(gz_recv.at[s], gz_ss.at[0], gz_rs.at[s]).wait_recv()

    total = gz_recv[0]
    for s in range(1, NZ):
        total = total + gz_recv[s]
    gb[...] = total
    along_y = z % 4 < 2
    at = jnp.where(along_y, y, x)
    for i in range(3):
        to = (at + OFFSETS[i]) % 4
        row = jnp.where(along_y, to * NX + x, y * NX + to)
        pending.append(send(gb.at[to], gb_recv.at[at], gb_ss.at[i], gb_rs.at[at], row, c))

    nf_out[:, 0 : MODE // 2] = dot3_t(inv_low, image)
    nf_out[:, MODE // 2 :] = dot3_t(inv_high, image)
    for oy, ox in PLANE:
        frm = plane(oy, ox)
        arrival(c_recv.at[frm], c_ss.at[0], c_rs.at[frm]).wait_recv()
    for s in range(NR):
        core_out[:, LANES * s : LANES * (s + 1)] = c_recv[s]

    total = gb[at]
    for i in range(3):
        frm = (at + OFFSETS[i]) % 4
        arrival(gb_recv.at[frm], gb_ss.at[0], gb_rs.at[frm]).wait_recv()
        total = total + gb_recv[frm]
    low_width = 128 * (r // 4 + 1)
    gfin[...] = jnp.zeros_like(gfin)
    gfin[:, 0:GW] = total
    owner = r * (NZ * NK) + c
    row_id = lax.broadcasted_iota(jnp.int32, (2, MODE), 0)
    col_id = lax.broadcasted_iota(jnp.int32, (2, MODE), 1)
    low = gfin[:, 0:MODE]
    high = gfin[:, pl.ds(pl.multiple_of(low_width, 128), MODE)]
    gram_out[0:2, :] = jnp.where(col_id <= 2 * owner + row_id, low, 0.0)
    gram_out[2:4, :] = jnp.where(col_id <= MODE - 2 - 2 * owner + row_id, high, 0.0)

    for copy in pending:
        copy.wait_send()
    for t in range(8):
        zz, kk = 4 * k + t // 2, t % 2

        @pl.when(jnp.logical_not(jnp.logical_and(zz == z, kk == k)))
        def _():
            arrival(gz_send.at[t], gz_ss.at[t], gz_rs.at[0]).wait_send()


def finish(gram_in, nf_in, core_in, gram_out, nf_out, core_out, sems):
    copies = []
    for i, (src, dst) in enumerate(((nf_in, nf_out), (core_in, core_out), (gram_in, gram_out))):
        copies.append(pltpu.make_async_copy(src, dst, sems.at[i]))
        copies[-1].start()
    for copy in copies:
        copy.wait()


def body(unfolding, factor):
    dma = pltpu.SemaphoreType.DMA
    hbm = functools.partial(pltpu.with_memory_space_constraint, memory_space=pltpu.HBM)
    vmem = pl.BlockSpec(memory_space=pltpu.VMEM)
    gram_lower, new_factor_t, core = pl.pallas_call(
        kernel,
        out_shape=(
            jax.ShapeDtypeStruct((4, MODE), F32),
            jax.ShapeDtypeStruct((RANK, MODE), F32),
            jax.ShapeDtypeStruct((RANK // NR, LANES * NR), F32),
        ),
        in_specs=[pl.BlockSpec(memory_space=pl.ANY)] * 2,
        out_specs=(vmem, vmem, vmem),
        scratch_shapes=[
            pltpu.VMEM((2, NR, ROWS, LANES), F32),
            pltpu.VMEM((RANK, MODE), F32),
            pltpu.VMEM((MODE // 2, 2 * LANES), F32),
            pltpu.VMEM((NR, NK, 16, 128), F32),
            pltpu.VMEM((NR * NK, 16, 128), F32),
            pltpu.VMEM((16, 128), F32),
            pltpu.VMEM((NZ, 16, 128), F32),
            pltpu.VMEM((16, 128), F32),
            pltpu.VMEM((NR * NK, 16, 128), F32),
            pltpu.VMEM((NR, RANK // NR, LANES), F32),
            pltpu.VMEM((NR, RANK // NR, LANES), F32),
            pltpu.VMEM((MODE // 2, 6 * LANES), BF16),
            pltpu.VMEM((MODE, 6 * LANES), BF16),
            pltpu.VMEM((2, 4, 4, 8, GW), F32),
            pltpu.VMEM((2, 4, 4, 8, GW), F32),
            pltpu.VMEM((4, 2, GW), F32),
            pltpu.VMEM((4, 2, GW), F32),
            pltpu.VMEM((8, 4, 2, GW), F32),
            pltpu.VMEM((NZ, 4, 2, GW), F32),
            pltpu.VMEM((2, 1536), F32),
            dma,
            dma,
            dma((NR - 1,)),
            dma((NR,)),
            dma,
            dma,
            dma((NR * NK - 1,)),
            dma((NR * NK,)),
            dma((NZ - 1,)),
            dma((NZ,)),
            dma((NR * NK - 1,)),
            dma((NR * NK,)),
            dma((NR - 1,)),
            dma((NR,)),
            dma((2, 3)),
            dma((2, 4)),
            dma((3,)),
            dma((4,)),
            dma((8,)),
            dma((NZ,)),
        ],
        compiler_params=pltpu.CompilerParams(
            collective_id=0, has_side_effects=True, vmem_limit_bytes=32 * 1024 * 1024
        ),
        name="tucker_update",
    )(hbm(unfolding), hbm(factor.T))
    anywhere = pl.BlockSpec(memory_space=pl.ANY)
    gram_lower, new_factor_t, core = pl.pallas_call(
        finish,
        out_shape=(
            jax.ShapeDtypeStruct((4, MODE), F32),
            jax.ShapeDtypeStruct((RANK, MODE), F32),
            jax.ShapeDtypeStruct((RANK // NR, LANES * NR), F32),
        ),
        in_specs=[anywhere, anywhere, anywhere],
        out_specs=(anywhere, anywhere, anywhere),
        scratch_shapes=[pltpu.SemaphoreType.DMA((3,))],
        compiler_params=pltpu.CompilerParams(vmem_limit_bytes=1024 * 1024),
        name="write_results",
    )(gram_lower, new_factor_t, core)
    return gram_lower, new_factor_t.T, core


def solution(mesh):
    in_specs = (P("row", "col"), P())
    out_specs = (P(("row", "col"), None), P(), P("row", "col"))
    return jax.shard_map(body, mesh=mesh, in_specs=in_specs, out_specs=out_specs, check_vma=False)
```

```python
import functools
import math

import jax
import jax.numpy as jnp
from jax import lax
from jax.experimental import pallas as pl
from jax.experimental.pallas import tpu as pltpu
from jax.sharding import PartitionSpec as P

F32 = jnp.float32
BF16 = jnp.bfloat16
HIGHEST = lax.Precision.HIGHEST
MESH = pl.DeviceIdType.MESH

NY, NX, NZ, NK = 4, 4, 8, 2
NR = NY * NX
MODE, RANK, COLS = 1024, 64, 32768
ROWS = MODE // NR
LANES = 128
GW = 1152

PLANE = [(oy, ox) for oy in range(NY) for ox in range(NX) if (oy, ox) != (0, 0)]
PLANE.sort(key=lambda o: -(min(o[0], NY - o[0]) + min(o[1], NX - o[1])))
PLANE_K = [(oy, ox, ok) for oy in range(NY) for ox in range(NX) for ok in range(NK)]
PLANE_K = [o for o in PLANE_K if o != (0, 0, 0)]
PLANE_K.sort(key=lambda o: -(min(o[0], NY - o[0]) + min(o[1], NX - o[1])))
OFFSETS = (1, 3, 2)
ZS = sorted(range(1, NZ), key=lambda o: -min(o, NZ - o))


def dot_t(a, b, precision=None):
    return lax.dot_general(
        a, b, (((1,), (1,)), ((), ())), precision=precision, preferred_element_type=F32
    )


def dot(a, b, precision=None):
    return lax.dot_general(
        a, b, (((1,), (0,)), ((), ())), precision=precision, preferred_element_type=F32
    )


def split(a):
    hi = a.astype(BF16)
    return hi, (a - hi.astype(F32)).astype(BF16)


def dot3(a, b):
    (ah, al), (bh, bl) = split(a), split(b)
    return dot(jnp.concatenate([ah, ah, al], axis=1), jnp.concatenate([bh, bl, bh], axis=0))


def dot3_t(a, b):
    (ah, al), (bh, bl) = split(a), split(b)
    return dot_t(jnp.concatenate([ah, ah, al], axis=1), jnp.concatenate([bh, bl, bh], axis=1))


def eliminate(inner):
    lane = lax.broadcasted_iota(jnp.int32, (8, 128), 1)
    sub = lax.broadcasted_iota(jnp.int32, (8, 128), 0)
    tiles = []
    for v in range(RANK // 8):
        unit = jnp.where(lane == sub + (8 * v + RANK), F32(1.0), F32(0.0))
        tiles.append(jnp.where(lane < RANK, inner[8 * v : 8 * v + 8, :], unit))

    def over_lanes(tile, j):
        return jnp.broadcast_to(tile[:, j : j + 1], (8, 128))

    def over_rows(tile, i):
        return jnp.broadcast_to(tile[i : i + 1, :], (8, 128))

    for v in range(RANK // 8):
        panel = tiles[v]
        spread = [over_lanes(panel, 8 * v + j) for j in range(8)]
        scale = jnp.ones((8, 128), F32)
        rows, links = [], []
        for s in range(8):
            pivot = over_rows(spread[s], s)
            inverse = 1.0 / pivot
            scale = jnp.where(sub == s, pivot, scale)
            row = over_rows(panel, s) * inverse
            link = [over_rows(spread[j], s) * inverse for j in range(s + 1, 8)]
            factor = jnp.where(sub > s, spread[s], 0.0)
            for j in range(s + 1, 8):
                spread[j] = spread[j] - factor * link[j - s - 1]
            panel = panel - factor * row
            rows.append(row)
            links.append(link)
        tiles[v] = panel * (1.0 / jnp.sqrt(scale))
        for w in range(v + 1, RANK // 8):
            spread = [over_lanes(tiles[w], 8 * v + j) for j in range(8)]
            for s in range(8):
                for j in range(s + 1, 8):
                    spread[j] = spread[j] - spread[s] * links[s][j - s - 1]
                tiles[w] = tiles[w] - spread[s] * rows[s]
    return jnp.concatenate([jnp.where(lane < RANK, 0.0, t) for t in tiles], axis=0)


def kernel(
    x_hbm,
    ft_hbm,
    gram_out,
    nf_out,
    core_out,
    xr,
    ft,
    xcat,
    img_send,
    img_recv,
    z_send,
    z_recv,
    p_send,
    p_all,
    c_send,
    c_recv,
    lhs,
    rhs,
    ga,
    ga_recv,
    gb,
    gb_recv,
    gz_send,
    gz_recv,
    gfin,
    own_sem,
    ft_sem,
    x_ss,
    x_rs,
    pair_ss,
    pair_rs,
    img_ss,
    img_rs,
    z_ss,
    z_rs,
    p_ss,
    p_rs,
    c_ss,
    c_rs,
    ga_ss,
    ga_rs,
    gb_ss,
    gb_rs,
    gz_ss,
    gz_rs,
):
    r = lax.axis_index("row")
    c = lax.axis_index("col")
    y, x = r // NX, r % NX
    z, k = c // NK, c % NK

    def plane(oy, ox):
        return ((y + oy) % NY) * NX + (x + ox) % NX

    def column(zz, kk):
        return zz * NK + kk

    def send(src, dst, ss, rs, row, col):
        copy = pltpu.make_async_remote_copy(
            src_ref=src,
            dst_ref=dst,
            send_sem=ss,
            recv_sem=rs,
            device_id=(row, col),
            device_id_type=MESH,
        )
        copy.start()
        return copy

    def arrival(dst, ss, rs):
        return pltpu.make_async_remote_copy(
            src_ref=dst,
            dst_ref=dst,
            send_sem=ss,
            recv_sem=rs,
            device_id=(r, c),
            device_id_type=MESH,
        )

    barrier = pltpu.get_barrier_semaphore()
    peers = 0
    for oy, ox, ok in PLANE_K:
        pl.semaphore_signal(
            barrier,
            inc=1,
            device_id=(plane(oy, ox), column(z, (k + ok) % NK)),
            device_id_type=MESH,
        )
        peers += 1
    for oz in ZS:
        for ok in range(NK):
            pl.semaphore_signal(
                barrier,
                inc=1,
                device_id=(r, column((z + oz) % NZ, (k + ok) % NK)),
                device_id_type=MESH,
            )
            peers += 1
    factor_copy = pltpu.make_async_copy(ft_hbm, ft, ft_sem)
    factor_copy.start()
    pl.semaphore_wait(barrier, peers)

    pending = []

    def columns_of(row):
        return pl.ds(pl.multiple_of(row * LANES, LANES), LANES)

    for oy, ox in PLANE:
        to = plane(oy, ox)
        send(x_hbm.at[:, columns_of(to)], xr.at[0, r], x_ss, x_rs, to, c)
    own = pltpu.make_async_copy(x_hbm.at[:, columns_of(r)], xr.at[0, r], own_sem)
    own.start()
    own.wait()
    factor_copy.wait()
    arrival(xr.at[0, 0 : NR - 1], x_ss, x_rs).wait_recv()
    partner = column(z, 1 - k)
    pending.append(send(xr.at[0], xr.at[1], pair_ss, pair_rs, r, partner))

    flat = xr[0].reshape(MODE, LANES)
    xcat[:, 0:LANES] = flat[0 : MODE // 2]
    xcat[:, LANES : 2 * LANES] = flat[MODE // 2 :]
    yt = dot3(ft[...], flat) * F32(1.0 / COLS)
    zero = jnp.zeros_like(yt)
    weights = jnp.concatenate(
        [jnp.concatenate([yt, zero], axis=1), jnp.concatenate([zero, yt], axis=1)], axis=0
    )
    term = dot3_t(xcat[...], weights)
    img_send[...] = term.reshape(NR, NK, 16, 128)
    me = r * NK + k
    for oy, ox, ok in PLANE_K:
        to, kk = plane(oy, ox), (k + ok) % NK
        send(img_send.at[to, kk], img_recv.at[me], img_ss, img_rs, to, column(z, kk))
    img_recv[me] = img_send[r, k]

    arrival(xr.at[1], pair_ss, pair_rs).wait_recv()
    for s in range(2):
        whole = xr[s].reshape(MODE, LANES)
        hi = whole.astype(BF16)
        lo = (whole - hi.astype(F32)).astype(BF16)
        rhs[:, s * LANES : (s + 1) * LANES] = hi
        rhs[:, (2 + s) * LANES : (3 + s) * LANES] = lo
        rhs[:, (4 + s) * LANES : (5 + s) * LANES] = hi
    for b in range(2 * NR):
        half = k if b < NR else 1 - k
        at = pl.ds(pl.multiple_of(32 * b + 16 * half, 16), 16)
        lhs[16 * b : 16 * b + 16, 0:256] = rhs[at, 0:256]
        lhs[16 * b : 16 * b + 16, 256:512] = rhs[at, 0:256]
        lhs[16 * b : 16 * b + 16, 512:768] = rhs[at, 256:512]
    at_row = lax.broadcasted_iota(jnp.int32, (256, 256), 0)
    at_col = lax.broadcasted_iota(jnp.int32, (256, 256), 1)
    mirrored = at_row - at_row % 16 + 14 - at_row % 16 + 2 * (at_row % 2)
    order = jnp.where(at_col == mirrored, F32(1.0), F32(0.0)).astype(BF16)
    lhs[256:512, 0:256] = dot(order, lhs[256:512, 0:256]).astype(BF16)
    lhs[256:512, 256:512] = lhs[256:512, 0:256]
    lhs[256:512, 512:768] = dot(order, lhs[256:512, 512:768]).astype(BF16)
    for nb in range(4):
        part = dot_t(lhs[128 * nb : 512, :], rhs[256 * nb : 256 * nb + 256, :]) * F32(1.0 / COLS)
        for b in range(8 * nb, 2 * NR):
            to = b if b < NR else 2 * NR - 1 - b
            off = 0 if b < NR else 128 * (8 - b // 4)
            width = min(256, 128 * (b // 4 + 1) - 256 * nb)
            rows_b = part[16 * (b - 8 * nb) : 16 * (b - 8 * nb) + 16, 0:width]
            at = pl.ds(off + 256 * nb, width)
            ga[0, to % NX, to // NX, :, at] = rows_b[0:8]
            ga[1, to // NX, to % NX, :, at] = rows_b[8:16]
    for i in range(3):
        xx, yy = (x + OFFSETS[i]) % NX, (y + OFFSETS[i]) % NY
        pending.append(
            send(ga.at[0, xx], ga_recv.at[0, x], ga_ss.at[0, i], ga_rs.at[0, x], y * NX + xx, c)
        )
        pending.append(
            send(ga.at[1, yy], ga_recv.at[1, y], ga_ss.at[1, i], ga_rs.at[1, y], yy * NX + x, c)
        )

    arrival(img_recv.at[0 : NR * NK - 1], img_ss, img_rs).wait_recv()
    total = img_recv[0]
    for s in range(1, NR * NK):
        total = total + img_recv[s]
    z_send[...] = total
    z_recv[z] = total
    for oz in ZS:
        send(z_send, z_recv.at[z], z_ss, z_rs, r, column((z + oz) % NZ, k))
    arrival(z_recv.at[0 : NZ - 1], z_ss, z_rs).wait_recv()
    total = z_recv[0]
    for s in range(1, NZ):
        total = total + z_recv[s]
    p_send[...] = total
    p_all[me] = total
    for oy, ox, ok in PLANE_K[::-1]:
        send(p_send, p_all.at[me], p_ss, p_rs, plane(oy, ox), column(z, (k + ok) % NK))

    for h, at in ((0, x), (1, y)):
        total = ga[h, at]
        for i in range(3):
            frm = (at + OFFSETS[i]) % 4
            arrival(ga_recv.at[h, frm], ga_ss.at[h, 0], ga_rs.at[h, frm]).wait_recv()
            total = total + ga_recv[h, frm]
        for t in range(4):
            gz_send[4 * h + t] = total[:, 2 * t : 2 * t + 2]
    for t in range(8):
        zz, kk = 4 * k + t // 2, t % 2
        mine = jnp.logical_and(zz == z, kk == k)

        @pl.when(jnp.logical_not(mine))
        def _():
            send(gz_send.at[t], gz_recv.at[z], gz_ss.at[t], gz_rs.at[z], r, column(zz, kk))

        @pl.when(mine)
        def _():
            gz_recv[z] = gz_send[t]

    arrival(p_all.at[0 : NR * NK - 1], p_ss, p_rs).wait_recv()

    image = p_all[...].reshape(MODE // 2, 128)
    image_t = image.T
    inner2 = dot3(image_t, image)
    products = dot3(image_t, xcat[...])
    inner = (inner2[0:RANK, :] + pltpu.roll(inner2[RANK:, :], RANK, 1)) * F32(1.0 / MODE)
    product = products[0:RANK, 0:LANES] + products[RANK:, LANES:]
    inv_high = eliminate(inner)
    inv_low = pltpu.roll(inv_high, RANK, 1)
    core = dot(inv_low[:, 0:RANK], product, HIGHEST) * F32(1.0 / math.sqrt(MODE))
    c_send[...] = core.reshape(NR, RANK // NR, LANES)
    for oy, ox in PLANE:
        to = plane(oy, ox)
        send(c_send.at[to], c_recv.at[r], c_ss, c_rs, to, c)
    c_recv[r] = c_send[r]

    from_core = z // 4
    for s in range(NZ):

        @pl.when(jnp.logical_not(jnp.logical_and(s == z, from_core == k)))
        def _():
            arrival(gz_recv.at[s], gz_ss.at[0], gz_rs.at[s]).wait_recv()

    total = gz_recv[0]
    for s in range(1, NZ):
        total = total + gz_recv[s]
    gb[...] = total
    along_y = z % 4 < 2
    at = jnp.where(along_y, y, x)
    for i in range(3):
        to = (at + OFFSETS[i]) % 4
        row = jnp.where(along_y, to * NX + x, y * NX + to)
        pending.append(send(gb.at[to], gb_recv.at[at], gb_ss.at[i], gb_rs.at[at], row, c))

    nf_out[:, 0 : MODE // 2] = dot3_t(inv_low, image)
    nf_out[:, MODE // 2 :] = dot3_t(inv_high, image)
    arrival(c_recv.at[0 : NR - 1], c_ss, c_rs).wait_recv()
    for s in range(NR):
        core_out[:, LANES * s : LANES * (s + 1)] = c_recv[s]

    total = gb[at]
    for i in range(3):
        frm = (at + OFFSETS[i]) % 4
        arrival(gb_recv.at[frm], gb_ss.at[0], gb_rs.at[frm]).wait_recv()
        total = total + gb_recv[frm]
    low_width = 128 * (r // 4 + 1)
    gfin[...] = jnp.zeros_like(gfin)
    gfin[:, 0:GW] = total
    owner = r * (NZ * NK) + c
    row_id = lax.broadcasted_iota(jnp.int32, (2, MODE), 0)
    col_id = lax.broadcasted_iota(jnp.int32, (2, MODE), 1)
    low = gfin[:, 0:MODE]
    high = gfin[:, pl.ds(pl.multiple_of(low_width, 128), MODE)]
    gram_out[0:2, :] = jnp.where(col_id <= 2 * owner + row_id, low, 0.0)
    gram_out[2:4, :] = jnp.where(col_id <= MODE - 2 - 2 * owner + row_id, high, 0.0)

    for copy in pending:
        copy.wait_send()
    arrival(xr.at[0, 0 : NR - 1], x_ss, x_rs).wait_send()
    arrival(img_recv.at[0 : NR * NK - 1], img_ss, img_rs).wait_send()
    arrival(z_recv.at[0 : NZ - 1], z_ss, z_rs).wait_send()
    arrival(p_all.at[0 : NR * NK - 1], p_ss, p_rs).wait_send()
    arrival(c_recv.at[0 : NR - 1], c_ss, c_rs).wait_send()
    for t in range(8):
        zz, kk = 4 * k + t // 2, t % 2

        @pl.when(jnp.logical_not(jnp.logical_and(zz == z, kk == k)))
        def _():
            arrival(gz_send.at[t], gz_ss.at[t], gz_rs.at[0]).wait_send()


def finish(gram_in, nf_in, core_in, gram_out, nf_out, core_out, sems):
    copies = []
    for i, (src, dst) in enumerate(((nf_in, nf_out), (core_in, core_out), (gram_in, gram_out))):
        copies.append(pltpu.make_async_copy(src, dst, sems.at[i]))
        copies[-1].start()
    for copy in copies:
        copy.wait()


def body(unfolding, factor):
    dma = pltpu.SemaphoreType.DMA
    hbm = functools.partial(pltpu.with_memory_space_constraint, memory_space=pltpu.HBM)
    vmem = pl.BlockSpec(memory_space=pltpu.VMEM)
    gram_lower, new_factor_t, core = pl.pallas_call(
        kernel,
        out_shape=(
            jax.ShapeDtypeStruct((4, MODE), F32),
            jax.ShapeDtypeStruct((RANK, MODE), F32),
            jax.ShapeDtypeStruct((RANK // NR, LANES * NR), F32),
        ),
        in_specs=[pl.BlockSpec(memory_space=pl.ANY)] * 2,
        out_specs=(vmem, vmem, vmem),
        scratch_shapes=[
            pltpu.VMEM((2, NR, ROWS, LANES), F32),
            pltpu.VMEM((RANK, MODE), F32),
            pltpu.VMEM((MODE // 2, 2 * LANES), F32),
            pltpu.VMEM((NR, NK, 16, 128), F32),
            pltpu.VMEM((NR * NK, 16, 128), F32),
            pltpu.VMEM((16, 128), F32),
            pltpu.VMEM((NZ, 16, 128), F32),
            pltpu.VMEM((16, 128), F32),
            pltpu.VMEM((NR * NK, 16, 128), F32),
            pltpu.VMEM((NR, RANK // NR, LANES), F32),
            pltpu.VMEM((NR, RANK // NR, LANES), F32),
            pltpu.VMEM((MODE // 2, 6 * LANES), BF16),
            pltpu.VMEM((MODE, 6 * LANES), BF16),
            pltpu.VMEM((2, 4, 4, 8, GW), F32),
            pltpu.VMEM((2, 4, 4, 8, GW), F32),
            pltpu.VMEM((4, 2, GW), F32),
            pltpu.VMEM((4, 2, GW), F32),
            pltpu.VMEM((8, 4, 2, GW), F32),
            pltpu.VMEM((NZ, 4, 2, GW), F32),
            pltpu.VMEM((2, 1536), F32),
            dma,
            dma,
            dma,
            dma,
            dma,
            dma,
            dma,
            dma,
            dma,
            dma,
            dma,
            dma,
            dma,
            dma,
            dma((2, 3)),
            dma((2, 4)),
            dma((3,)),
            dma((4,)),
            dma((8,)),
            dma((NZ,)),
        ],
        compiler_params=pltpu.CompilerParams(
            collective_id=0, has_side_effects=True, vmem_limit_bytes=32 * 1024 * 1024
        ),
        name="tucker_update",
    )(hbm(unfolding), hbm(factor.T))
    anywhere = pl.BlockSpec(memory_space=pl.ANY)
    gram_lower, new_factor_t, core = pl.pallas_call(
        finish,
        out_shape=(
            jax.ShapeDtypeStruct((4, MODE), F32),
            jax.ShapeDtypeStruct((RANK, MODE), F32),
            jax.ShapeDtypeStruct((RANK // NR, LANES * NR), F32),
        ),
        in_specs=[anywhere, anywhere, anywhere],
        out_specs=(anywhere, anywhere, anywhere),
        scratch_shapes=[pltpu.SemaphoreType.DMA((3,))],
        compiler_params=pltpu.CompilerParams(vmem_limit_bytes=1024 * 1024),
        name="write_results",
    )(gram_lower, new_factor_t, core)
    return gram_lower, new_factor_t.T, core


def solution(mesh):
    in_specs = (P("row", "col"), P())
    out_specs = (P(("row", "col"), None), P(), P("row", "col"))
    return jax.shard_map(body, mesh=mesh, in_specs=in_specs, out_specs=out_specs, check_vma=False)
```

```python
import functools
import math

import jax
import jax.numpy as jnp
from jax import lax
from jax.experimental import pallas as pl
from jax.experimental.pallas import tpu as pltpu
from jax.sharding import PartitionSpec as P

F32 = jnp.float32
BF16 = jnp.bfloat16
HIGHEST = lax.Precision.HIGHEST
MESH = pl.DeviceIdType.MESH

NY, NX, NZ, NK = 4, 4, 8, 2
NR = NY * NX
MODE, RANK, COLS = 1024, 64, 32768
ROWS = MODE // NR
LANES = 128
GW = 1152

PLANE = [(oy, ox) for oy in range(NY) for ox in range(NX) if (oy, ox) != (0, 0)]
PLANE.sort(key=lambda o: -(min(o[0], NY - o[0]) + min(o[1], NX - o[1])))
PLANE_K = [(oy, ox, ok) for oy in range(NY) for ox in range(NX) for ok in range(NK)]
PLANE_K = [o for o in PLANE_K if o != (0, 0, 0)]
PLANE_K.sort(key=lambda o: -(min(o[0], NY - o[0]) + min(o[1], NX - o[1])))
OFFSETS = (1, 3, 2)
ZS = sorted(range(1, NZ), key=lambda o: -min(o, NZ - o))


def dot_t(a, b, precision=None):
    return lax.dot_general(
        a, b, (((1,), (1,)), ((), ())), precision=precision, preferred_element_type=F32
    )


def dot(a, b, precision=None):
    return lax.dot_general(
        a, b, (((1,), (0,)), ((), ())), precision=precision, preferred_element_type=F32
    )


def split(a):
    hi = a.astype(BF16)
    return hi, (a - hi.astype(F32)).astype(BF16)


def dot3(a, b):
    (ah, al), (bh, bl) = split(a), split(b)
    return dot(jnp.concatenate([ah, ah, al], axis=1), jnp.concatenate([bh, bl, bh], axis=0))


def dot3_t(a, b):
    (ah, al), (bh, bl) = split(a), split(b)
    return dot_t(jnp.concatenate([ah, ah, al], axis=1), jnp.concatenate([bh, bl, bh], axis=1))


def eliminate(inner):
    lane = lax.broadcasted_iota(jnp.int32, (8, 128), 1)
    sub = lax.broadcasted_iota(jnp.int32, (8, 128), 0)
    tiles = []
    for v in range(RANK // 8):
        unit = jnp.where(lane == sub + (8 * v + RANK), F32(1.0), F32(0.0))
        tiles.append(jnp.where(lane < RANK, inner[8 * v : 8 * v + 8, :], unit))

    def over_lanes(tile, j):
        return jnp.broadcast_to(tile[:, j : j + 1], (8, 128))

    def over_rows(tile, i):
        return jnp.broadcast_to(tile[i : i + 1, :], (8, 128))

    for v in range(RANK // 8):
        panel = tiles[v]
        spread = [over_lanes(panel, 8 * v + j) for j in range(8)]
        scale = jnp.ones((8, 128), F32)
        rows, links = [], []
        for s in range(8):
            pivot = over_rows(spread[s], s)
            inverse = 1.0 / pivot
            scale = jnp.where(sub == s, pivot, scale)
            row = over_rows(panel, s) * inverse
            link = [over_rows(spread[j], s) * inverse for j in range(s + 1, 8)]
            factor = jnp.where(sub > s, spread[s], 0.0)
            for j in range(s + 1, 8):
                spread[j] = spread[j] - factor * link[j - s - 1]
            panel = panel - factor * row
            rows.append(row)
            links.append(link)
        tiles[v] = panel * (1.0 / jnp.sqrt(scale))
        for w in range(v + 1, RANK // 8):
            spread = [over_lanes(tiles[w], 8 * v + j) for j in range(8)]
            for s in range(8):
                for j in range(s + 1, 8):
                    spread[j] = spread[j] - spread[s] * links[s][j - s - 1]
                tiles[w] = tiles[w] - spread[s] * rows[s]
    return jnp.concatenate([jnp.where(lane < RANK, 0.0, t) for t in tiles], axis=0)


def kernel(
    x_hbm,
    ft_hbm,
    gram_out,
    nf_out,
    core_out,
    xr,
    ft,
    xcat,
    img_send,
    img_recv,
    z_send,
    z_recv,
    p_send,
    p_all,
    c_send,
    c_recv,
    lhs,
    rhs,
    ga,
    ga_recv,
    gb,
    gb_recv,
    gz_send,
    gz_recv,
    gfin,
    own_sem,
    ft_sem,
    x_ss,
    x_rs,
    pair_ss,
    pair_rs,
    img_ss,
    img_rs,
    z_ss,
    z_rs,
    p_ss,
    p_rs,
    c_ss,
    c_rs,
    ga_ss,
    ga_rs,
    gb_ss,
    gb_rs,
    gz_ss,
    gz_rs,
):
    r = lax.axis_index("row")
    c = lax.axis_index("col")
    y, x = r // NX, r % NX
    z, k = c // NK, c % NK

    def plane(oy, ox):
        return ((y + oy) % NY) * NX + (x + ox) % NX

    def column(zz, kk):
        return zz * NK + kk

    def send(src, dst, ss, rs, row, col):
        copy = pltpu.make_async_remote_copy(
            src_ref=src,
            dst_ref=dst,
            send_sem=ss,
            recv_sem=rs,
            device_id=(row, col),
            device_id_type=MESH,
        )
        copy.start()
        return copy

    def arrival(dst, ss, rs):
        return pltpu.make_async_remote_copy(
            src_ref=dst,
            dst_ref=dst,
            send_sem=ss,
            recv_sem=rs,
            device_id=(r, c),
            device_id_type=MESH,
        )

    barrier = pltpu.get_barrier_semaphore()
    peers = 0
    for oy, ox, ok in PLANE_K:
        pl.semaphore_signal(
            barrier,
            inc=1,
            device_id=(plane(oy, ox), column(z, (k + ok) % NK)),
            device_id_type=MESH,
        )
        peers += 1
    for oz in ZS:
        for ok in range(NK):
            pl.semaphore_signal(
                barrier,
                inc=1,
                device_id=(r, column((z + oz) % NZ, (k + ok) % NK)),
                device_id_type=MESH,
            )
            peers += 1
    factor_copy = pltpu.make_async_copy(ft_hbm, ft, ft_sem)
    factor_copy.start()
    pl.semaphore_wait(barrier, peers)

    pending = []

    def columns_of(row):
        return pl.ds(pl.multiple_of(row * LANES, LANES), LANES)

    for oy, ox in PLANE:
        to = plane(oy, ox)
        send(x_hbm.at[:, columns_of(to)], xr.at[0, r], x_ss, x_rs, to, c)
    own = pltpu.make_async_copy(x_hbm.at[:, columns_of(r)], xr.at[0, r], own_sem)
    own.start()
    own.wait()
    factor_copy.wait()
    arrival(xr.at[0, 0 : NR - 1], x_ss, x_rs).wait_recv()
    partner = column(z, 1 - k)
    pending.append(send(xr.at[0], xr.at[1], pair_ss, pair_rs, r, partner))

    flat = xr[0].reshape(MODE, LANES)
    xcat[:, 0:LANES] = flat[0 : MODE // 2]
    xcat[:, LANES : 2 * LANES] = flat[MODE // 2 :]
    yt = dot3(ft[...], flat) * F32(1.0 / COLS)
    zero = jnp.zeros_like(yt)
    weights = jnp.concatenate(
        [jnp.concatenate([yt, zero], axis=1), jnp.concatenate([zero, yt], axis=1)], axis=0
    )
    me = r * NK + k
    wh, wl = split(weights)
    wcat = jnp.concatenate([wh, wl, wh], axis=1)
    for group in ((2, 1), (3, 0)):
        for oy in group:
            yy = (y + oy) % NY
            ah, al = split(xcat[pl.ds(pl.multiple_of(yy * 128, 128), 128), :])
            term = dot_t(jnp.concatenate([ah, ah, al], axis=1), wcat)
            img_send[pl.ds(yy * NX, NX)] = term.reshape(NX, NK, 16, 128)
        for oy, ox, ok in PLANE_K:
            if oy in group:
                to, kk = plane(oy, ox), (k + ok) % NK
                send(img_send.at[to, kk], img_recv.at[me], img_ss, img_rs, to, column(z, kk))
    img_recv[me] = img_send[r, k]

    arrival(xr.at[1], pair_ss, pair_rs).wait_recv()
    for s in range(2):
        whole = xr[s].reshape(MODE, LANES)
        hi = whole.astype(BF16)
        lo = (whole - hi.astype(F32)).astype(BF16)
        rhs[:, s * LANES : (s + 1) * LANES] = hi
        rhs[:, (2 + s) * LANES : (3 + s) * LANES] = lo
        rhs[:, (4 + s) * LANES : (5 + s) * LANES] = hi
    for b in range(2 * NR):
        half = k if b < NR else 1 - k
        at = pl.ds(pl.multiple_of(32 * b + 16 * half, 16), 16)
        lhs[16 * b : 16 * b + 16, 0:256] = rhs[at, 0:256]
        lhs[16 * b : 16 * b + 16, 256:512] = rhs[at, 0:256]
        lhs[16 * b : 16 * b + 16, 512:768] = rhs[at, 256:512]
    at_row = lax.broadcasted_iota(jnp.int32, (256, 256), 0)
    at_col = lax.broadcasted_iota(jnp.int32, (256, 256), 1)
    mirrored = at_row - at_row % 16 + 14 - at_row % 16 + 2 * (at_row % 2)
    order = jnp.where(at_col == mirrored, F32(1.0), F32(0.0)).astype(BF16)
    lhs[256:512, 0:256] = dot(order, lhs[256:512, 0:256]).astype(BF16)
    lhs[256:512, 256:512] = lhs[256:512, 0:256]
    lhs[256:512, 512:768] = dot(order, lhs[256:512, 512:768]).astype(BF16)
    for nb in range(4):
        part = dot_t(lhs[128 * nb : 512, :], rhs[256 * nb : 256 * nb + 256, :]) * F32(1.0 / COLS)
        for b in range(8 * nb, 2 * NR):
            to = b if b < NR else 2 * NR - 1 - b
            off = 0 if b < NR else 128 * (8 - b // 4)
            width = min(256, 128 * (b // 4 + 1) - 256 * nb)
            rows_b = part[16 * (b - 8 * nb) : 16 * (b - 8 * nb) + 16, 0:width]
            at = pl.ds(off + 256 * nb, width)
            ga[0, to % NX, to // NX, :, at] = rows_b[0:8]
            ga[1, to // NX, to % NX, :, at] = rows_b[8:16]
    for i in range(3):
        xx, yy = (x + OFFSETS[i]) % NX, (y + OFFSETS[i]) % NY
        send(ga.at[0, xx], ga_recv.at[0, x], ga_ss.at[0], ga_rs.at[0], y * NX + xx, c)
        send(ga.at[1, yy], ga_recv.at[1, y], ga_ss.at[1], ga_rs.at[1], yy * NX + x, c)

    arrival(img_recv.at[0 : NR * NK - 1], img_ss, img_rs).wait_recv()
    total = img_recv[0]
    for s in range(1, NR * NK):
        total = total + img_recv[s]
    z_send[...] = total
    z_recv[z] = total
    for oz in ZS:
        send(z_send, z_recv.at[z], z_ss, z_rs, r, column((z + oz) % NZ, k))
    arrival(z_recv.at[0 : NZ - 1], z_ss, z_rs).wait_recv()
    total = z_recv[0]
    for s in range(1, NZ):
        total = total + z_recv[s]
    p_send[...] = total
    p_all[me] = total
    for oy, ox, ok in PLANE_K[::-1]:
        send(p_send, p_all.at[me], p_ss, p_rs, plane(oy, ox), column(z, (k + ok) % NK))

    for h, at in ((0, x), (1, y)):
        arrival(ga_recv.at[h, 0:3], ga_ss.at[h], ga_rs.at[h]).wait_recv()
        total = ga[h, at]
        for i in range(3):
            total = total + ga_recv[h, (at + OFFSETS[i]) % 4]
        for t in range(4):
            gz_send[4 * h + t] = total[:, 2 * t : 2 * t + 2]
    for t in range(8):
        zz, kk = 4 * k + t // 2, t % 2
        mine = jnp.logical_and(zz == z, kk == k)

        @pl.when(jnp.logical_not(mine))
        def _():
            send(gz_send.at[t], gz_recv.at[z], gz_ss, gz_rs, r, column(zz, kk))

        @pl.when(mine)
        def _():
            gz_recv[z] = gz_send[t]

    arrival(p_all.at[0 : NR * NK - 1], p_ss, p_rs).wait_recv()

    image = p_all[...].reshape(MODE // 2, 128)
    image_t = image.T
    inner2 = dot3(image_t, image)
    products = dot3(image_t, xcat[...])
    inner = (inner2[0:RANK, :] + pltpu.roll(inner2[RANK:, :], RANK, 1)) * F32(1.0 / MODE)
    product = products[0:RANK, 0:LANES] + products[RANK:, LANES:]
    inv_high = eliminate(inner)
    inv_low = pltpu.roll(inv_high, RANK, 1)
    core = dot(inv_low[:, 0:RANK], product, HIGHEST) * F32(1.0 / math.sqrt(MODE))
    c_send[...] = core.reshape(NR, RANK // NR, LANES)
    for oy, ox in PLANE:
        to = plane(oy, ox)
        send(c_send.at[to], c_recv.at[r], c_ss, c_rs, to, c)
    c_recv[r] = c_send[r]

    from_core = z // 4

    @pl.when(from_core == k)
    def _():
        arrival(gz_recv.at[0 : NZ - 1], gz_ss, gz_rs).wait_recv()

    @pl.when(from_core != k)
    def _():
        arrival(gz_recv, gz_ss, gz_rs).wait_recv()

    total = gz_recv[0]
    for s in range(1, NZ):
        total = total + gz_recv[s]
    gb[...] = total
    along_y = z % 4 < 2
    at = jnp.where(along_y, y, x)
    for i in range(3):
        to = (at + OFFSETS[i]) % 4
        row = jnp.where(along_y, to * NX + x, y * NX + to)
        send(gb.at[to], gb_recv.at[at], gb_ss, gb_rs, row, c)

    nf_out[:, 0 : MODE // 2] = dot3_t(inv_low, image)
    nf_out[:, MODE // 2 :] = dot3_t(inv_high, image)
    arrival(c_recv.at[0 : NR - 1], c_ss, c_rs).wait_recv()
    for s in range(NR):
        core_out[:, LANES * s : LANES * (s + 1)] = c_recv[s]

    arrival(gb_recv.at[0:3], gb_ss, gb_rs).wait_recv()
    total = gb[at]
    for i in range(3):
        total = total + gb_recv[(at + OFFSETS[i]) % 4]
    low_width = 128 * (r // 4 + 1)
    gfin[...] = jnp.zeros_like(gfin)
    gfin[:, 0:GW] = total
    owner = r * (NZ * NK) + c
    row_id = lax.broadcasted_iota(jnp.int32, (2, MODE), 0)
    col_id = lax.broadcasted_iota(jnp.int32, (2, MODE), 1)
    low = gfin[:, 0:MODE]
    high = gfin[:, pl.ds(pl.multiple_of(low_width, 128), MODE)]
    gram_out[0:2, :] = jnp.where(col_id <= 2 * owner + row_id, low, 0.0)
    gram_out[2:4, :] = jnp.where(col_id <= MODE - 2 - 2 * owner + row_id, high, 0.0)

    for copy in pending:
        copy.wait_send()
    arrival(xr.at[0, 0 : NR - 1], x_ss, x_rs).wait_send()
    arrival(img_recv.at[0 : NR * NK - 1], img_ss, img_rs).wait_send()
    arrival(z_recv.at[0 : NZ - 1], z_ss, z_rs).wait_send()
    arrival(p_all.at[0 : NR * NK - 1], p_ss, p_rs).wait_send()
    arrival(c_recv.at[0 : NR - 1], c_ss, c_rs).wait_send()
    arrival(ga_recv.at[0, 0:3], ga_ss.at[0], ga_rs.at[0]).wait_send()
    arrival(ga_recv.at[1, 0:3], ga_ss.at[1], ga_rs.at[1]).wait_send()
    arrival(gb_recv.at[0:3], gb_ss, gb_rs).wait_send()

    @pl.when(from_core == k)
    def _():
        arrival(gz_recv.at[0 : NZ - 1], gz_ss, gz_rs).wait_send()

    @pl.when(from_core != k)
    def _():
        arrival(gz_recv, gz_ss, gz_rs).wait_send()


def finish(gram_in, nf_in, core_in, gram_out, nf_out, core_out, sems):
    copies = []
    for i, (src, dst) in enumerate(((nf_in, nf_out), (core_in, core_out), (gram_in, gram_out))):
        copies.append(pltpu.make_async_copy(src, dst, sems.at[i]))
        copies[-1].start()
    for copy in copies:
        copy.wait()


def body(unfolding, factor):
    dma = pltpu.SemaphoreType.DMA
    hbm = functools.partial(pltpu.with_memory_space_constraint, memory_space=pltpu.HBM)
    vmem = pl.BlockSpec(memory_space=pltpu.VMEM)
    gram_lower, new_factor_t, core = pl.pallas_call(
        kernel,
        out_shape=(
            jax.ShapeDtypeStruct((4, MODE), F32),
            jax.ShapeDtypeStruct((RANK, MODE), F32),
            jax.ShapeDtypeStruct((RANK // NR, LANES * NR), F32),
        ),
        in_specs=[pl.BlockSpec(memory_space=pl.ANY)] * 2,
        out_specs=(vmem, vmem, vmem),
        scratch_shapes=[
            pltpu.VMEM((2, NR, ROWS, LANES), F32),
            pltpu.VMEM((RANK, MODE), F32),
            pltpu.VMEM((MODE // 2, 2 * LANES), F32),
            pltpu.VMEM((NR, NK, 16, 128), F32),
            pltpu.VMEM((NR * NK, 16, 128), F32),
            pltpu.VMEM((16, 128), F32),
            pltpu.VMEM((NZ, 16, 128), F32),
            pltpu.VMEM((16, 128), F32),
            pltpu.VMEM((NR * NK, 16, 128), F32),
            pltpu.VMEM((NR, RANK // NR, LANES), F32),
            pltpu.VMEM((NR, RANK // NR, LANES), F32),
            pltpu.VMEM((MODE // 2, 6 * LANES), BF16),
            pltpu.VMEM((MODE, 6 * LANES), BF16),
            pltpu.VMEM((2, 4, 4, 8, GW), F32),
            pltpu.VMEM((2, 4, 4, 8, GW), F32),
            pltpu.VMEM((4, 2, GW), F32),
            pltpu.VMEM((4, 2, GW), F32),
            pltpu.VMEM((8, 4, 2, GW), F32),
            pltpu.VMEM((NZ, 4, 2, GW), F32),
            pltpu.VMEM((2, 1536), F32),
            dma,
            dma,
            dma,
            dma,
            dma,
            dma,
            dma,
            dma,
            dma,
            dma,
            dma,
            dma,
            dma,
            dma,
            dma((2,)),
            dma((2,)),
            dma,
            dma,
            dma,
            dma,
        ],
        compiler_params=pltpu.CompilerParams(
            collective_id=0, has_side_effects=True, vmem_limit_bytes=32 * 1024 * 1024
        ),
        name="tucker_update",
    )(hbm(unfolding), hbm(factor.T))
    anywhere = pl.BlockSpec(memory_space=pl.ANY)
    gram_lower, new_factor_t, core = pl.pallas_call(
        finish,
        out_shape=(
            jax.ShapeDtypeStruct((4, MODE), F32),
            jax.ShapeDtypeStruct((RANK, MODE), F32),
            jax.ShapeDtypeStruct((RANK // NR, LANES * NR), F32),
        ),
        in_specs=[anywhere, anywhere, anywhere],
        out_specs=(anywhere, anywhere, anywhere),
        scratch_shapes=[pltpu.SemaphoreType.DMA((3,))],
        compiler_params=pltpu.CompilerParams(vmem_limit_bytes=1024 * 1024),
        name="write_results",
    )(gram_lower, new_factor_t, core)
    return gram_lower, new_factor_t.T, core


def solution(mesh):
    in_specs = (P("row", "col"), P())
    out_specs = (P(("row", "col"), None), P(), P("row", "col"))
    return jax.shard_map(body, mesh=mesh, in_specs=in_specs, out_specs=out_specs, check_vma=False)
```

```python
import functools
import math

import jax
import jax.numpy as jnp
from jax import lax
from jax.experimental import pallas as pl
from jax.experimental.pallas import tpu as pltpu
from jax.sharding import PartitionSpec as P

F32 = jnp.float32
BF16 = jnp.bfloat16
HIGHEST = lax.Precision.HIGHEST
MESH = pl.DeviceIdType.MESH

NY, NX, NZ, NK = 4, 4, 8, 2
NR = NY * NX
MODE, RANK, COLS = 1024, 64, 32768
ROWS = MODE // NR
LANES = 128
GW = 1152

PLANE = [(oy, ox) for oy in range(NY) for ox in range(NX) if (oy, ox) != (0, 0)]
PLANE.sort(key=lambda o: -(min(o[0], NY - o[0]) + min(o[1], NX - o[1])))
PLANE_K = [(oy, ox, ok) for oy in range(NY) for ox in range(NX) for ok in range(NK)]
PLANE_K = [o for o in PLANE_K if o != (0, 0, 0)]
PLANE_K.sort(key=lambda o: -(min(o[0], NY - o[0]) + min(o[1], NX - o[1])))
OFFSETS = (1, 3, 2)
ZS = sorted(range(1, NZ), key=lambda o: -min(o, NZ - o))


def dot_t(a, b, precision=None):
    return lax.dot_general(
        a, b, (((1,), (1,)), ((), ())), precision=precision, preferred_element_type=F32
    )


def dot(a, b, precision=None):
    return lax.dot_general(
        a, b, (((1,), (0,)), ((), ())), precision=precision, preferred_element_type=F32
    )


def split(a):
    hi = a.astype(BF16)
    return hi, (a - hi.astype(F32)).astype(BF16)


def dot3(a, b):
    (ah, al), (bh, bl) = split(a), split(b)
    return dot(jnp.concatenate([ah, ah, al], axis=1), jnp.concatenate([bh, bl, bh], axis=0))


def dot3_t(a, b):
    (ah, al), (bh, bl) = split(a), split(b)
    return dot_t(jnp.concatenate([ah, ah, al], axis=1), jnp.concatenate([bh, bl, bh], axis=1))


def eliminate(inner):
    lane = lax.broadcasted_iota(jnp.int32, (8, 128), 1)
    sub = lax.broadcasted_iota(jnp.int32, (8, 128), 0)
    tiles = []
    for v in range(RANK // 8):
        unit = jnp.where(lane == sub + (8 * v + RANK), F32(1.0), F32(0.0))
        tiles.append(jnp.where(lane < RANK, inner[8 * v : 8 * v + 8, :], unit))

    def over_lanes(tile, j):
        return jnp.broadcast_to(tile[:, j : j + 1], (8, 128))

    def over_rows(tile, i):
        return jnp.broadcast_to(tile[i : i + 1, :], (8, 128))

    for v in range(RANK // 8):
        panel = tiles[v]
        spread = [over_lanes(panel, 8 * v + j) for j in range(8)]
        scale = jnp.ones((8, 128), F32)
        rows, links = [], []
        for s in range(8):
            pivot = over_rows(spread[s], s)
            inverse = 1.0 / pivot
            scale = jnp.where(sub == s, pivot, scale)
            row = over_rows(panel, s) * inverse
            link = [over_rows(spread[j], s) * inverse for j in range(s + 1, 8)]
            factor = jnp.where(sub > s, spread[s], 0.0)
            for j in range(s + 1, 8):
                spread[j] = spread[j] - factor * link[j - s - 1]
            panel = panel - factor * row
            rows.append(row)
            links.append(link)
        tiles[v] = panel * (1.0 / jnp.sqrt(scale))
        for w in range(v + 1, RANK // 8):
            spread = [over_lanes(tiles[w], 8 * v + j) for j in range(8)]
            for s in range(8):
                for j in range(s + 1, 8):
                    spread[j] = spread[j] - spread[s] * links[s][j - s - 1]
                tiles[w] = tiles[w] - spread[s] * rows[s]
    return jnp.concatenate([jnp.where(lane < RANK, 0.0, t) for t in tiles], axis=0)


def kernel(
    x_hbm,
    ft_hbm,
    gram_out,
    nf_out,
    core_out,
    xr,
    ft,
    xcat,
    img_send,
    img_recv,
    z_send,
    z_recv,
    p_send,
    p_all,
    c_send,
    c_recv,
    lhs,
    rhs,
    ga,
    ga_recv,
    gb,
    gb_recv,
    gz_send,
    gz_recv,
    gfin,
    own_sem,
    ft_sem,
    x_ss,
    x_rs,
    pair_ss,
    pair_rs,
    img_ss,
    img_rs,
    z_ss,
    z_rs,
    p_ss,
    p_rs,
    c_ss,
    c_rs,
    ga_ss,
    ga_rs,
    gb_ss,
    gb_rs,
    gz_ss,
    gz_rs,
):
    r = lax.axis_index("row")
    c = lax.axis_index("col")
    y, x = r // NX, r % NX
    z, k = c // NK, c % NK

    def plane(oy, ox):
        return ((y + oy) % NY) * NX + (x + ox) % NX

    def column(zz, kk):
        return zz * NK + kk

    def send(src, dst, ss, rs, row, col):
        copy = pltpu.make_async_remote_copy(
            src_ref=src,
            dst_ref=dst,
            send_sem=ss,
            recv_sem=rs,
            device_id=(row, col),
            device_id_type=MESH,
        )
        copy.start()
        return copy

    def arrival(dst, ss, rs):
        return pltpu.make_async_remote_copy(
            src_ref=dst,
            dst_ref=dst,
            send_sem=ss,
            recv_sem=rs,
            device_id=(r, c),
            device_id_type=MESH,
        )

    barrier = pltpu.get_barrier_semaphore()
    peers = 0
    for oy, ox, ok in PLANE_K:
        pl.semaphore_signal(
            barrier,
            inc=1,
            device_id=(plane(oy, ox), column(z, (k + ok) % NK)),
            device_id_type=MESH,
        )
        peers += 1
    for oz in ZS:
        for ok in range(NK):
            pl.semaphore_signal(
                barrier,
                inc=1,
                device_id=(r, column((z + oz) % NZ, (k + ok) % NK)),
                device_id_type=MESH,
            )
            peers += 1
    factor_copy = pltpu.make_async_copy(ft_hbm, ft, ft_sem)
    factor_copy.start()
    pl.semaphore_wait(barrier, peers)

    pending = []

    def columns_of(row):
        return pl.ds(pl.multiple_of(row * LANES, LANES), LANES)

    for oy, ox in PLANE:
        to = plane(oy, ox)
        send(x_hbm.at[:, columns_of(to)], xr.at[0, r], x_ss, x_rs, to, c)
    own = pltpu.make_async_copy(x_hbm.at[:, columns_of(r)], xr.at[0, r], own_sem)
    own.start()
    own.wait()
    factor_copy.wait()
    arrival(xr.at[0, 0 : NR - 1], x_ss, x_rs).wait_recv()
    partner = column(z, 1 - k)
    pending.append(send(xr.at[0], xr.at[1], pair_ss, pair_rs, r, partner))

    flat = xr[0].reshape(MODE, LANES)
    xcat[:, 0:LANES] = flat[0 : MODE // 2]
    xcat[:, LANES : 2 * LANES] = flat[MODE // 2 :]
    yt = dot3(ft[...], flat) * F32(1.0 / COLS)
    zero = jnp.zeros_like(yt)
    weights = jnp.concatenate(
        [jnp.concatenate([yt, zero], axis=1), jnp.concatenate([zero, yt], axis=1)], axis=0
    )
    me = r * NK + k
    wh, wl = split(weights)
    wcat = jnp.concatenate([wh, wl, wh], axis=1)
    for group in ((2, 1), (3, 0)):
        for oy in group:
            yy = (y + oy) % NY
            ah, al = split(xcat[pl.ds(pl.multiple_of(yy * 128, 128), 128), :])
            term = dot_t(jnp.concatenate([ah, ah, al], axis=1), wcat)
            img_send[pl.ds(yy * NX, NX)] = term.reshape(NX, NK, 16, 128)
        for oy, ox, ok in PLANE_K:
            if oy in group:
                to, kk = plane(oy, ox), (k + ok) % NK
                send(img_send.at[to, kk], img_recv.at[me], img_ss, img_rs, to, column(z, kk))
    img_recv[me] = img_send[r, k]

    arrival(xr.at[1], pair_ss, pair_rs).wait_recv()
    for s in range(2):
        whole = xr[s].reshape(MODE, LANES)
        hi = whole.astype(BF16)
        lo = (whole - hi.astype(F32)).astype(BF16)
        rhs[:, s * LANES : (s + 1) * LANES] = hi
        rhs[:, (2 + s) * LANES : (3 + s) * LANES] = lo
        rhs[:, (4 + s) * LANES : (5 + s) * LANES] = hi
    for b in range(2 * NR):
        half = k if b < NR else 1 - k
        at = pl.ds(pl.multiple_of(32 * b + 16 * half, 16), 16)
        lhs[16 * b : 16 * b + 16, 0:256] = rhs[at, 0:256]
        lhs[16 * b : 16 * b + 16, 256:512] = rhs[at, 0:256]
        lhs[16 * b : 16 * b + 16, 512:768] = rhs[at, 256:512]
    at_row = lax.broadcasted_iota(jnp.int32, (256, 256), 0)
    at_col = lax.broadcasted_iota(jnp.int32, (256, 256), 1)
    mirrored = at_row - at_row % 16 + 14 - at_row % 16 + 2 * (at_row % 2)
    order = jnp.where(at_col == mirrored, F32(1.0), F32(0.0)).astype(BF16)
    lhs[256:512, 0:256] = dot(order, lhs[256:512, 0:256]).astype(BF16)
    lhs[256:512, 256:512] = lhs[256:512, 0:256]
    lhs[256:512, 512:768] = dot(order, lhs[256:512, 512:768]).astype(BF16)
    for nb in range(4):
        part = dot_t(lhs[128 * nb : 512, :], rhs[256 * nb : 256 * nb + 256, :]) * F32(1.0 / COLS)
        for b in range(8 * nb, 2 * NR):
            to = b if b < NR else 2 * NR - 1 - b
            off = 0 if b < NR else 128 * (8 - b // 4)
            width = min(256, 128 * (b // 4 + 1) - 256 * nb)
            rows_b = part[16 * (b - 8 * nb) : 16 * (b - 8 * nb) + 16, 0:width]
            at = pl.ds(off + 256 * nb, width)
            ga[0, to % NX, to // NX, :, at] = rows_b[0:8]
            ga[1, to // NX, to % NX, :, at] = rows_b[8:16]
    for i in range(3):
        xx, yy = (x + OFFSETS[i]) % NX, (y + OFFSETS[i]) % NY
        send(ga.at[0, xx], ga_recv.at[0, x], ga_ss.at[0], ga_rs.at[0], y * NX + xx, c)
        send(ga.at[1, yy], ga_recv.at[1, y], ga_ss.at[1], ga_rs.at[1], yy * NX + x, c)

    arrival(img_recv.at[0 : NR * NK - 1], img_ss, img_rs).wait_recv()
    total = img_recv[0]
    for s in range(1, NR * NK):
        total = total + img_recv[s]
    z_send[...] = total
    z_recv[z] = total
    for oz in ZS:
        send(z_send, z_recv.at[z], z_ss, z_rs, r, column((z + oz) % NZ, k))
    arrival(z_recv.at[0 : NZ - 1], z_ss, z_rs).wait_recv()
    total = z_recv[0]
    for s in range(1, NZ):
        total = total + z_recv[s]
    p_send[...] = total
    p_all[me] = total
    for oy, ox, ok in PLANE_K[::-1]:
        send(p_send, p_all.at[me], p_ss, p_rs, plane(oy, ox), column(z, (k + ok) % NK))

    for h, at in ((0, x), (1, y)):
        arrival(ga_recv.at[h, 0:3], ga_ss.at[h], ga_rs.at[h]).wait_recv()
        total = ga[h, at]
        for i in range(3):
            total = total + ga_recv[h, (at + OFFSETS[i]) % 4]
        for t in range(4):
            gz_send[4 * h + t] = total[:, 2 * t : 2 * t + 2]
    for t in range(8):
        zz, kk = 4 * k + t // 2, t % 2
        mine = jnp.logical_and(zz == z, kk == k)

        @pl.when(jnp.logical_not(mine))
        def _():
            send(gz_send.at[t], gz_recv.at[z], gz_ss, gz_rs, r, column(zz, kk))

        @pl.when(mine)
        def _():
            gz_recv[z] = gz_send[t]

    arrival(p_all.at[0 : NR * NK - 1], p_ss, p_rs).wait_recv()

    image = p_all[...].reshape(MODE // 2, 128)
    image_t = image.T
    inner2 = dot3(image_t, image)
    products = dot3(image_t, xcat[...])
    inner = (inner2[0:RANK, :] + pltpu.roll(inner2[RANK:, :], RANK, 1)) * F32(1.0 / MODE)
    product = products[0:RANK, 0:LANES] + products[RANK:, LANES:]
    inv_high = eliminate(inner)
    inv_low = pltpu.roll(inv_high, RANK, 1)
    core = dot(inv_low[:, 0:RANK], product, HIGHEST) * F32(1.0 / math.sqrt(MODE))
    c_send[...] = core.reshape(NR, RANK // NR, LANES)
    for oy, ox in PLANE:
        to = plane(oy, ox)
        send(c_send.at[to], c_recv.at[r], c_ss, c_rs, to, c)
    c_recv[r] = c_send[r]

    from_core = z // 4

    @pl.when(from_core == k)
    def _():
        arrival(gz_recv.at[0 : NZ - 1], gz_ss, gz_rs).wait_recv()

    @pl.when(from_core != k)
    def _():
        arrival(gz_recv, gz_ss, gz_rs).wait_recv()

    total = gz_recv[0]
    for s in range(1, NZ):
        total = total + gz_recv[s]
    gb[...] = total
    along_y = z % 4 < 2
    at = jnp.where(along_y, y, x)
    for i in range(3):
        to = (at + OFFSETS[i]) % 4
        row = jnp.where(along_y, to * NX + x, y * NX + to)
        send(gb.at[to], gb_recv.at[at], gb_ss, gb_rs, row, c)

    nf_out[:, 0 : MODE // 2] = dot3_t(inv_low, image)
    nf_out[:, MODE // 2 :] = dot3_t(inv_high, image)
    arrival(gb_recv.at[0:3], gb_ss, gb_rs).wait_recv()
    total = gb[at]
    for i in range(3):
        total = total + gb_recv[(at + OFFSETS[i]) % 4]
    low_width = 128 * (r // 4 + 1)
    gfin[...] = jnp.zeros_like(gfin)
    gfin[:, 0:GW] = total
    owner = r * (NZ * NK) + c
    row_id = lax.broadcasted_iota(jnp.int32, (2, MODE), 0)
    col_id = lax.broadcasted_iota(jnp.int32, (2, MODE), 1)
    low = gfin[:, 0:MODE]
    high = gfin[:, pl.ds(pl.multiple_of(low_width, 128), MODE)]
    gram_out[0:2, :] = jnp.where(col_id <= 2 * owner + row_id, low, 0.0)
    gram_out[2:4, :] = jnp.where(col_id <= MODE - 2 - 2 * owner + row_id, high, 0.0)

    arrival(c_recv.at[0 : NR - 1], c_ss, c_rs).wait_recv()
    for s in range(NR):
        core_out[:, LANES * s : LANES * (s + 1)] = c_recv[s]

    for copy in pending:
        copy.wait_send()
    arrival(xr.at[0, 0 : NR - 1], x_ss, x_rs).wait_send()
    arrival(img_recv.at[0 : NR * NK - 1], img_ss, img_rs).wait_send()
    arrival(z_recv.at[0 : NZ - 1], z_ss, z_rs).wait_send()
    arrival(p_all.at[0 : NR * NK - 1], p_ss, p_rs).wait_send()
    arrival(c_recv.at[0 : NR - 1], c_ss, c_rs).wait_send()
    arrival(ga_recv.at[0, 0:3], ga_ss.at[0], ga_rs.at[0]).wait_send()
    arrival(ga_recv.at[1, 0:3], ga_ss.at[1], ga_rs.at[1]).wait_send()
    arrival(gb_recv.at[0:3], gb_ss, gb_rs).wait_send()

    @pl.when(from_core == k)
    def _():
        arrival(gz_recv.at[0 : NZ - 1], gz_ss, gz_rs).wait_send()

    @pl.when(from_core != k)
    def _():
        arrival(gz_recv, gz_ss, gz_rs).wait_send()


def finish(gram_in, nf_in, core_in, gram_out, nf_out, core_out, sems):
    copies = []
    for i, (src, dst) in enumerate(((nf_in, nf_out), (core_in, core_out), (gram_in, gram_out))):
        copies.append(pltpu.make_async_copy(src, dst, sems.at[i]))
        copies[-1].start()
    for copy in copies:
        copy.wait()


def body(unfolding, factor):
    dma = pltpu.SemaphoreType.DMA
    hbm = functools.partial(pltpu.with_memory_space_constraint, memory_space=pltpu.HBM)
    vmem = pl.BlockSpec(memory_space=pltpu.VMEM)
    gram_lower, new_factor_t, core = pl.pallas_call(
        kernel,
        out_shape=(
            jax.ShapeDtypeStruct((4, MODE), F32),
            jax.ShapeDtypeStruct((RANK, MODE), F32),
            jax.ShapeDtypeStruct((RANK // NR, LANES * NR), F32),
        ),
        in_specs=[pl.BlockSpec(memory_space=pl.ANY)] * 2,
        out_specs=(vmem, vmem, vmem),
        scratch_shapes=[
            pltpu.VMEM((2, NR, ROWS, LANES), F32),
            pltpu.VMEM((RANK, MODE), F32),
            pltpu.VMEM((MODE // 2, 2 * LANES), F32),
            pltpu.VMEM((NR, NK, 16, 128), F32),
            pltpu.VMEM((NR * NK, 16, 128), F32),
            pltpu.VMEM((16, 128), F32),
            pltpu.VMEM((NZ, 16, 128), F32),
            pltpu.VMEM((16, 128), F32),
            pltpu.VMEM((NR * NK, 16, 128), F32),
            pltpu.VMEM((NR, RANK // NR, LANES), F32),
            pltpu.VMEM((NR, RANK // NR, LANES), F32),
            pltpu.VMEM((MODE // 2, 6 * LANES), BF16),
            pltpu.VMEM((MODE, 6 * LANES), BF16),
            pltpu.VMEM((2, 4, 4, 8, GW), F32),
            pltpu.VMEM((2, 4, 4, 8, GW), F32),
            pltpu.VMEM((4, 2, GW), F32),
            pltpu.VMEM((4, 2, GW), F32),
            pltpu.VMEM((8, 4, 2, GW), F32),
            pltpu.VMEM((NZ, 4, 2, GW), F32),
            pltpu.VMEM((2, 1536), F32),
            dma,
            dma,
            dma,
            dma,
            dma,
            dma,
            dma,
            dma,
            dma,
            dma,
            dma,
            dma,
            dma,
            dma,
            dma((2,)),
            dma((2,)),
            dma,
            dma,
            dma,
            dma,
        ],
        compiler_params=pltpu.CompilerParams(
            collective_id=0, has_side_effects=True, vmem_limit_bytes=32 * 1024 * 1024
        ),
        name="tucker_update",
    )(hbm(unfolding), hbm(factor.T))
    anywhere = pl.BlockSpec(memory_space=pl.ANY)
    gram_lower, new_factor_t, core = pl.pallas_call(
        finish,
        out_shape=(
            jax.ShapeDtypeStruct((4, MODE), F32),
            jax.ShapeDtypeStruct((RANK, MODE), F32),
            jax.ShapeDtypeStruct((RANK // NR, LANES * NR), F32),
        ),
        in_specs=[anywhere, anywhere, anywhere],
        out_specs=(anywhere, anywhere, anywhere),
        scratch_shapes=[pltpu.SemaphoreType.DMA((3,))],
        compiler_params=pltpu.CompilerParams(vmem_limit_bytes=1024 * 1024),
        name="write_results",
    )(gram_lower, new_factor_t, core)
    return gram_lower, new_factor_t.T, core


def solution(mesh):
    in_specs = (P("row", "col"), P())
    out_specs = (P(("row", "col"), None), P(), P("row", "col"))
    return jax.shard_map(body, mesh=mesh, in_specs=in_specs, out_specs=out_specs, check_vma=False)
```

```python
import functools
import math

import jax
import jax.numpy as jnp
from jax import lax
from jax.experimental import pallas as pl
from jax.experimental.pallas import tpu as pltpu
from jax.sharding import PartitionSpec as P

F32 = jnp.float32
BF16 = jnp.bfloat16
HIGHEST = lax.Precision.HIGHEST
MESH = pl.DeviceIdType.MESH

NY, NX, NZ, NK = 4, 4, 8, 2
NR = NY * NX
MODE, RANK, COLS = 1024, 64, 32768
ROWS = MODE // NR
LANES = 128
GW = 1152

PLANE = [(oy, ox) for oy in range(NY) for ox in range(NX) if (oy, ox) != (0, 0)]
PLANE.sort(key=lambda o: -(min(o[0], NY - o[0]) + min(o[1], NX - o[1])))
PLANE_K = [(oy, ox, ok) for oy in range(NY) for ox in range(NX) for ok in range(NK)]
PLANE_K = [o for o in PLANE_K if o != (0, 0, 0)]
PLANE_K.sort(key=lambda o: -(min(o[0], NY - o[0]) + min(o[1], NX - o[1])))
OFFSETS = (1, 3, 2)
ZS = sorted(range(1, NZ), key=lambda o: -min(o, NZ - o))


def dot_t(a, b, precision=None):
    return lax.dot_general(
        a, b, (((1,), (1,)), ((), ())), precision=precision, preferred_element_type=F32
    )


def dot(a, b, precision=None):
    return lax.dot_general(
        a, b, (((1,), (0,)), ((), ())), precision=precision, preferred_element_type=F32
    )


def split(a):
    hi = a.astype(BF16)
    return hi, (a - hi.astype(F32)).astype(BF16)


def dot3(a, b):
    (ah, al), (bh, bl) = split(a), split(b)
    return dot(jnp.concatenate([ah, ah, al], axis=1), jnp.concatenate([bh, bl, bh], axis=0))


def dot3_t(a, b):
    (ah, al), (bh, bl) = split(a), split(b)
    return dot_t(jnp.concatenate([ah, ah, al], axis=1), jnp.concatenate([bh, bl, bh], axis=1))


def eliminate(inner):
    lane = lax.broadcasted_iota(jnp.int32, (8, 128), 1)
    sub = lax.broadcasted_iota(jnp.int32, (8, 128), 0)
    tiles = []
    for v in range(RANK // 8):
        unit = jnp.where(lane == sub + (8 * v + RANK), F32(1.0), F32(0.0))
        tiles.append(jnp.where(lane < RANK, inner[8 * v : 8 * v + 8, :], unit))

    def over_lanes(tile, j):
        return jnp.broadcast_to(tile[:, j : j + 1], (8, 128))

    def over_rows(tile, i):
        return jnp.broadcast_to(tile[i : i + 1, :], (8, 128))

    for v in range(RANK // 8):
        panel = tiles[v]
        spread = [over_lanes(panel, 8 * v + j) for j in range(8)]
        scale = jnp.ones((8, 128), F32)
        rows, links = [], []
        for s in range(8):
            pivot = over_rows(spread[s], s)
            inverse = 1.0 / pivot
            scale = jnp.where(sub == s, pivot, scale)
            row = over_rows(panel, s) * inverse
            link = [over_rows(spread[j], s) * inverse for j in range(s + 1, 8)]
            factor = jnp.where(sub > s, spread[s], 0.0)
            for j in range(s + 1, 8):
                spread[j] = spread[j] - factor * link[j - s - 1]
            panel = panel - factor * row
            rows.append(row)
            links.append(link)
        tiles[v] = panel * (1.0 / jnp.sqrt(scale))
        for w in range(v + 1, RANK // 8):
            spread = [over_lanes(tiles[w], 8 * v + j) for j in range(8)]
            for s in range(8):
                for j in range(s + 1, 8):
                    spread[j] = spread[j] - spread[s] * links[s][j - s - 1]
                tiles[w] = tiles[w] - spread[s] * rows[s]
    return jnp.concatenate([jnp.where(lane < RANK, 0.0, t) for t in tiles], axis=0)


def kernel(
    x_hbm,
    ft_hbm,
    gram_out,
    nf_out,
    core_out,
    xr,
    ft,
    xcat,
    img_send,
    img_recv,
    z_send,
    z_recv,
    p_send,
    p_all,
    c_send,
    c_recv,
    lhs,
    rhs,
    ga,
    ga_recv,
    gb,
    gb_recv,
    gz_send,
    gz_recv,
    gfin,
    own_sem,
    ft_sem,
    x_ss,
    x_rs,
    pair_ss,
    pair_rs,
    img_ss,
    img_rs,
    z_ss,
    z_rs,
    p_ss,
    p_rs,
    c_ss,
    c_rs,
    ga_ss,
    ga_rs,
    gb_ss,
    gb_rs,
    gz_ss,
    gz_rs,
):
    r = lax.axis_index("row")
    c = lax.axis_index("col")
    y, x = r // NX, r % NX
    z, k = c // NK, c % NK

    def plane(oy, ox):
        return ((y + oy) % NY) * NX + (x + ox) % NX

    def column(zz, kk):
        return zz * NK + kk

    def send(src, dst, ss, rs, row, col):
        copy = pltpu.make_async_remote_copy(
            src_ref=src,
            dst_ref=dst,
            send_sem=ss,
            recv_sem=rs,
            device_id=(row, col),
            device_id_type=MESH,
        )
        copy.start()
        return copy

    def arrival(dst, ss, rs):
        return pltpu.make_async_remote_copy(
            src_ref=dst,
            dst_ref=dst,
            send_sem=ss,
            recv_sem=rs,
            device_id=(r, c),
            device_id_type=MESH,
        )

    barrier = pltpu.get_barrier_semaphore()
    peers = 0
    for oy, ox, ok in PLANE_K:
        pl.semaphore_signal(
            barrier,
            inc=1,
            device_id=(plane(oy, ox), column(z, (k + ok) % NK)),
            device_id_type=MESH,
        )
        peers += 1
    for oz in ZS:
        for ok in range(NK):
            pl.semaphore_signal(
                barrier,
                inc=1,
                device_id=(r, column((z + oz) % NZ, (k + ok) % NK)),
                device_id_type=MESH,
            )
            peers += 1
    factor_copy = pltpu.make_async_copy(ft_hbm, ft, ft_sem)
    factor_copy.start()
    pl.semaphore_wait(barrier, peers)

    pending = []

    def columns_of(row):
        return pl.ds(pl.multiple_of(row * LANES, LANES), LANES)

    for oy, ox in PLANE:
        to = plane(oy, ox)
        send(x_hbm.at[:, columns_of(to)], xr.at[0, r], x_ss, x_rs, to, c)
    own = pltpu.make_async_copy(x_hbm.at[:, columns_of(r)], xr.at[0, r], own_sem)
    own.start()
    own.wait()
    factor_copy.wait()
    arrival(xr.at[0, 0 : NR - 1], x_ss, x_rs).wait_recv()
    partner = column(z, 1 - k)
    pending.append(send(xr.at[0], xr.at[1], pair_ss, pair_rs, r, partner))

    flat = xr[0].reshape(MODE, LANES)
    xcat[:, 0:LANES] = flat[0 : MODE // 2]
    xcat[:, LANES : 2 * LANES] = flat[MODE // 2 :]
    yt = dot3(ft[...], flat) * F32(1.0 / COLS)
    zero = jnp.zeros_like(yt)
    weights = jnp.concatenate(
        [jnp.concatenate([yt, zero], axis=1), jnp.concatenate([zero, yt], axis=1)], axis=0
    )
    me = r * NK + k
    wh, wl = split(weights)
    wcat = jnp.concatenate([wh, wl, wh], axis=1)
    for group in ((2, 1), (3, 0)):
        for oy in group:
            yy = (y + oy) % NY
            ah, al = split(xcat[pl.ds(pl.multiple_of(yy * 128, 128), 128), :])
            term = dot_t(jnp.concatenate([ah, ah, al], axis=1), wcat)
            img_send[pl.ds(yy * NX, NX)] = term.reshape(NX, NK, 16, 128)
        for oy, ox, ok in PLANE_K:
            if oy in group:
                to, kk = plane(oy, ox), (k + ok) % NK
                send(img_send.at[to, kk], img_recv.at[me], img_ss, img_rs, to, column(z, kk))
    img_recv[me] = img_send[r, k]

    arrival(xr.at[1], pair_ss, pair_rs).wait_recv()
    for s in range(2):
        whole = xr[s].reshape(MODE, LANES)
        hi = whole.astype(BF16)
        lo = (whole - hi.astype(F32)).astype(BF16)
        rhs[:, s * LANES : (s + 1) * LANES] = hi
        rhs[:, (2 + s) * LANES : (3 + s) * LANES] = lo
        rhs[:, (4 + s) * LANES : (5 + s) * LANES] = hi
    for b in range(2 * NR):
        half = k if b < NR else 1 - k
        at = pl.ds(pl.multiple_of(32 * b + 16 * half, 16), 16)
        lhs[16 * b : 16 * b + 16, 0:256] = rhs[at, 0:256]
        lhs[16 * b : 16 * b + 16, 256:512] = rhs[at, 0:256]
        lhs[16 * b : 16 * b + 16, 512:768] = rhs[at, 256:512]
    at_row = lax.broadcasted_iota(jnp.int32, (256, 256), 0)
    at_col = lax.broadcasted_iota(jnp.int32, (256, 256), 1)
    mirrored = at_row - at_row % 16 + 14 - at_row % 16 + 2 * (at_row % 2)
    order = jnp.where(at_col == mirrored, F32(1.0), F32(0.0)).astype(BF16)
    lhs[256:512, 0:256] = dot(order, lhs[256:512, 0:256]).astype(BF16)
    lhs[256:512, 256:512] = lhs[256:512, 0:256]
    lhs[256:512, 512:768] = dot(order, lhs[256:512, 512:768]).astype(BF16)
    for nb in range(4):
        part = dot_t(lhs[128 * nb : 512, :], rhs[256 * nb : 256 * nb + 256, :]) * F32(1.0 / COLS)
        for b in range(8 * nb, 2 * NR):
            to = b if b < NR else 2 * NR - 1 - b
            off = 0 if b < NR else 128 * (8 - b // 4)
            width = min(256, 128 * (b // 4 + 1) - 256 * nb)
            rows_b = part[16 * (b - 8 * nb) : 16 * (b - 8 * nb) + 16, 0:width]
            at = pl.ds(off + 256 * nb, width)
            ga[0, to % NX, to // NX, :, at] = rows_b[0:8]
            ga[1, to // NX, to % NX, :, at] = rows_b[8:16]
    for i in range(3):
        xx, yy = (x + OFFSETS[i]) % NX, (y + OFFSETS[i]) % NY
        send(ga.at[0, xx], ga_recv.at[0, x], ga_ss.at[0], ga_rs.at[0], y * NX + xx, c)
        send(ga.at[1, yy], ga_recv.at[1, y], ga_ss.at[1], ga_rs.at[1], yy * NX + x, c)

    arrival(img_recv.at[0 : NR * NK - 1], img_ss, img_rs).wait_recv()
    total = img_recv[0]
    for s in range(1, NR * NK):
        total = total + img_recv[s]
    z_send[...] = total
    z_recv[z] = total
    for oz in ZS:
        send(z_send, z_recv.at[z], z_ss, z_rs, r, column((z + oz) % NZ, k))
    arrival(z_recv.at[0 : NZ - 1], z_ss, z_rs).wait_recv()
    total = z_recv[0]
    for s in range(1, NZ):
        total = total + z_recv[s]
    p_send[...] = total
    p_all[me] = total
    for oy, ox, ok in PLANE_K[::-1]:
        send(p_send, p_all.at[me], p_ss, p_rs, plane(oy, ox), column(z, (k + ok) % NK))

    for h, at in ((0, x), (1, y)):
        arrival(ga_recv.at[h, 0:3], ga_ss.at[h], ga_rs.at[h]).wait_recv()
        total = ga[h, at]
        for i in range(3):
            total = total + ga_recv[h, (at + OFFSETS[i]) % 4]
        for t in range(4):
            gz_send[4 * h + t] = total[:, 2 * t : 2 * t + 2]
    for t in range(8):
        zz, kk = 4 * k + t // 2, t % 2
        mine = jnp.logical_and(zz == z, kk == k)

        @pl.when(jnp.logical_not(mine))
        def _():
            send(gz_send.at[t], gz_recv.at[z], gz_ss, gz_rs, r, column(zz, kk))

        @pl.when(mine)
        def _():
            gz_recv[z] = gz_send[t]

    arrival(p_all.at[0 : NR * NK - 1], p_ss, p_rs).wait_recv()

    image = p_all[...].reshape(MODE // 2, 128)
    image_t = image.T
    inner2 = dot3(image_t, image)
    products = dot3(image_t, xcat[...])
    inner = (inner2[0:RANK, :] + pltpu.roll(inner2[RANK:, :], RANK, 1)) * F32(1.0 / MODE)
    product = products[0:RANK, 0:LANES] + products[RANK:, LANES:]
    inv_high = eliminate(inner)
    inv_low = pltpu.roll(inv_high, RANK, 1)
    core = dot3(inv_low[:, 0:RANK], product) * F32(1.0 / math.sqrt(MODE))
    c_send[...] = core.reshape(NR, RANK // NR, LANES)
    for oy, ox in PLANE:
        to = plane(oy, ox)
        send(c_send.at[to], c_recv.at[r], c_ss, c_rs, to, c)
    c_recv[r] = c_send[r]

    from_core = z // 4

    @pl.when(from_core == k)
    def _():
        arrival(gz_recv.at[0 : NZ - 1], gz_ss, gz_rs).wait_recv()

    @pl.when(from_core != k)
    def _():
        arrival(gz_recv, gz_ss, gz_rs).wait_recv()

    total = gz_recv[0]
    for s in range(1, NZ):
        total = total + gz_recv[s]
    gb[...] = total
    along_y = z % 4 < 2
    at = jnp.where(along_y, y, x)
    for i in range(3):
        to = (at + OFFSETS[i]) % 4
        row = jnp.where(along_y, to * NX + x, y * NX + to)
        send(gb.at[to], gb_recv.at[at], gb_ss, gb_rs, row, c)

    nf_out[:, 0 : MODE // 2] = dot3_t(inv_low, image)
    nf_out[:, MODE // 2 :] = dot3_t(inv_high, image)
    arrival(gb_recv.at[0:3], gb_ss, gb_rs).wait_recv()
    total = gb[at]
    for i in range(3):
        total = total + gb_recv[(at + OFFSETS[i]) % 4]
    low_width = 128 * (r // 4 + 1)
    gfin[...] = jnp.zeros_like(gfin)
    gfin[:, 0:GW] = total
    owner = r * (NZ * NK) + c
    row_id = lax.broadcasted_iota(jnp.int32, (2, MODE), 0)
    col_id = lax.broadcasted_iota(jnp.int32, (2, MODE), 1)
    low = gfin[:, 0:MODE]
    high = gfin[:, pl.ds(pl.multiple_of(low_width, 128), MODE)]
    gram_out[0:2, :] = jnp.where(col_id <= 2 * owner + row_id, low, 0.0)
    gram_out[2:4, :] = jnp.where(col_id <= MODE - 2 - 2 * owner + row_id, high, 0.0)

    arrival(c_recv.at[0 : NR - 1], c_ss, c_rs).wait_recv()
    for s in range(NR):
        core_out[:, LANES * s : LANES * (s + 1)] = c_recv[s]

    for copy in pending:
        copy.wait_send()
    arrival(xr.at[0, 0 : NR - 1], x_ss, x_rs).wait_send()
    arrival(img_recv.at[0 : NR * NK - 1], img_ss, img_rs).wait_send()
    arrival(z_recv.at[0 : NZ - 1], z_ss, z_rs).wait_send()
    arrival(p_all.at[0 : NR * NK - 1], p_ss, p_rs).wait_send()
    arrival(c_recv.at[0 : NR - 1], c_ss, c_rs).wait_send()
    arrival(ga_recv.at[0, 0:3], ga_ss.at[0], ga_rs.at[0]).wait_send()
    arrival(ga_recv.at[1, 0:3], ga_ss.at[1], ga_rs.at[1]).wait_send()
    arrival(gb_recv.at[0:3], gb_ss, gb_rs).wait_send()

    @pl.when(from_core == k)
    def _():
        arrival(gz_recv.at[0 : NZ - 1], gz_ss, gz_rs).wait_send()

    @pl.when(from_core != k)
    def _():
        arrival(gz_recv, gz_ss, gz_rs).wait_send()


def finish(gram_in, nf_in, core_in, gram_out, nf_out, core_out, sems):
    copies = []
    for i, (src, dst) in enumerate(((nf_in, nf_out), (core_in, core_out), (gram_in, gram_out))):
        copies.append(pltpu.make_async_copy(src, dst, sems.at[i]))
        copies[-1].start()
    for copy in copies:
        copy.wait()


def body(unfolding, factor):
    dma = pltpu.SemaphoreType.DMA
    hbm = functools.partial(pltpu.with_memory_space_constraint, memory_space=pltpu.HBM)
    vmem = pl.BlockSpec(memory_space=pltpu.VMEM)
    gram_lower, new_factor_t, core = pl.pallas_call(
        kernel,
        out_shape=(
            jax.ShapeDtypeStruct((4, MODE), F32),
            jax.ShapeDtypeStruct((RANK, MODE), F32),
            jax.ShapeDtypeStruct((RANK // NR, LANES * NR), F32),
        ),
        in_specs=[pl.BlockSpec(memory_space=pl.ANY)] * 2,
        out_specs=(vmem, vmem, vmem),
        scratch_shapes=[
            pltpu.VMEM((2, NR, ROWS, LANES), F32),
            pltpu.VMEM((RANK, MODE), F32),
            pltpu.VMEM((MODE // 2, 2 * LANES), F32),
            pltpu.VMEM((NR, NK, 16, 128), F32),
            pltpu.VMEM((NR * NK, 16, 128), F32),
            pltpu.VMEM((16, 128), F32),
            pltpu.VMEM((NZ, 16, 128), F32),
            pltpu.VMEM((16, 128), F32),
            pltpu.VMEM((NR * NK, 16, 128), F32),
            pltpu.VMEM((NR, RANK // NR, LANES), F32),
            pltpu.VMEM((NR, RANK // NR, LANES), F32),
            pltpu.VMEM((MODE // 2, 6 * LANES), BF16),
            pltpu.VMEM((MODE, 6 * LANES), BF16),
            pltpu.VMEM((2, 4, 4, 8, GW), F32),
            pltpu.VMEM((2, 4, 4, 8, GW), F32),
            pltpu.VMEM((4, 2, GW), F32),
            pltpu.VMEM((4, 2, GW), F32),
            pltpu.VMEM((8, 4, 2, GW), F32),
            pltpu.VMEM((NZ, 4, 2, GW), F32),
            pltpu.VMEM((2, 1536), F32),
            dma,
            dma,
            dma,
            dma,
            dma,
            dma,
            dma,
            dma,
            dma,
            dma,
            dma,
            dma,
            dma,
            dma,
            dma((2,)),
            dma((2,)),
            dma,
            dma,
            dma,
            dma,
        ],
        compiler_params=pltpu.CompilerParams(
            collective_id=0, has_side_effects=True, vmem_limit_bytes=32 * 1024 * 1024
        ),
        name="tucker_update",
    )(hbm(unfolding), hbm(factor.T))
    anywhere = pl.BlockSpec(memory_space=pl.ANY)
    gram_lower, new_factor_t, core = pl.pallas_call(
        finish,
        out_shape=(
            jax.ShapeDtypeStruct((4, MODE), F32),
            jax.ShapeDtypeStruct((RANK, MODE), F32),
            jax.ShapeDtypeStruct((RANK // NR, LANES * NR), F32),
        ),
        in_specs=[anywhere, anywhere, anywhere],
        out_specs=(anywhere, anywhere, anywhere),
        scratch_shapes=[pltpu.SemaphoreType.DMA((3,))],
        compiler_params=pltpu.CompilerParams(vmem_limit_bytes=1024 * 1024),
        name="write_results",
    )(gram_lower, new_factor_t, core)
    return gram_lower, new_factor_t.T, core


def solution(mesh):
    in_specs = (P("row", "col"), P())
    out_specs = (P(("row", "col"), None), P(), P("row", "col"))
    return jax.shard_map(body, mesh=mesh, in_specs=in_specs, out_specs=out_specs, check_vma=False)
```
